256 devices in a mesh: section: 8 (over z), expert: 16 (over y, x), dp: 2 (over core).
Axes of the slice: x: 4, y: 4, z: 8, core: 2. Of those that a mesh axis runs over, the one named last changes fastest.
Arguments:
- stash: bfloat16 [8, 256, 2048], P('section', 'dp', 'expert'), may hold values from -6 to 6
- cotangent: bfloat16 [8, 256, 2048], P('section', 'dp', 'expert'), may hold values from -6 to 6
- backward_expert_routes: int32 [8, 256, 2], P('section', 'dp'), may hold values from 0 to 3, all different within a row; in each aligned block of 128 rows (0 to 127, 128 to 255, ..., all dimensions but the last counted through in order) at most 80 rows name the same one
- backward_job_lengths: int32 [8, 4], P('section'), may hold values from 1 to 128, 256 in all within a row
- layer_norm_gains: float32 [8, 2048], P('section'), may hold values from 0.25 to 1.75
- router: bfloat16 [8, 2048, 4], P('section'), may hold values from -0.125 to 0.125
- expert_gate_weight: bfloat16 [8, 2048, 28672], P('section', None, ('expert', 'dp')), may hold values from -0.125 to 0.125
- expert_up_weight: bfloat16 [8, 2048, 28672], P('section', None, ('expert', 'dp')), may hold values from -0.125 to 0.125
- expert_down_weight: bfloat16 [8, 28672, 2048], P('section', ('expert', 'dp')), may hold values from -0.0625 to 0.0625
- adapter_down_maps: bfloat16 [8, 2048, 64], P('section', 'expert'), may hold values from -0.125 to 0.125
- adapter_up_maps: bfloat16 [8, 64, 2048], P('section', None, 'expert'), may hold values from -1.5 to 1.5
Outputs:
- handed_back: bfloat16 [8, 256, 2048], P('section', 'dp', 'expert')
- grad_lora_down: float32 [8, 2048, 64], P('section', 'expert')
- grad_lora_up: float32 [8, 64, 2048], P('section', None, 'expert')
The draws below stay inside these ranges and needn't reach their ends.
Inputs may be any that keep to these rules, and one draw needn't show every extreme that they name: `backward_expert_routes`: each row names two different experts. In each aligned block of 128 rows (the tokens of one device) no expert is named more than 80 times. `backward_job_lengths`: each row sums to 256.
All inputs are finite; a program needn't handle non-finite values.
Results may differ from the reference program's by a relative error of at most 0.008.
Values may be sent and summed in bfloat16 or wider, within the bound.
No kernel may reach another device: no remote copies, remote signals or barrier semaphores. Data moves between devices by JAX's collectives and lax.ppermute only.
A program may use at most 64 MiB of HBM per device.

```python
import math
import jax
import jax.numpy as jnp
import numpy as np
from jax import lax

MODEL_WIDTH = 2048
FF = 7168
EXPERTS = 4
TOP = 2
ADAPTER_RANK = 16
ADAPTER_JOBS = 4
TOK_DEV = 128
CAP = 80
TOKENS = 256
LAYER_COUNT = 8


def levels(rng, dims, split, low, top_value):
    def one(dim, blocks):
        steps = jax.random.uniform(jax.random.fold_in(jax.random.fold_in(rng, 6), dim), (blocks,), jnp.float32, low / len(split), top_value / len(split))
        return jnp.repeat(jnp.exp(steps), dims[dim] // blocks).reshape((-1,) + (1,) * (len(dims) - dim - 1))

    level = one(*split[0])
    for cut in split[1:]:
        level = level * one(*cut)
    return level


def profile(count, total, reach, lean):
    weights = [(1 << 20) // math.isqrt(rank ** lean) + 1 for rank in range(2, count + 1)]
    spare, given = total - reach - (count - 1), [1] * (count - 1)
    while spare > 0:
        candidates = [i for i in range(count - 1) if given[i] < reach]
        pool, budget = sum([weights[i] for i in candidates]), spare
        for i in candidates:
            extra = min(reach - given[i], max(1, budget * weights[i] // pool), spare)
            given[i] = given[i] + extra
            spare = spare - extra
    return np.array([reach] + given)


def uneven(rng, number_of, total, reach, lean):
    if number_of == 2:
        one = jax.random.randint(rng, (), max(1, total - reach), min(reach, total - 1) + 1)
        return jnp.stack([one, total - one])
    lengths = jnp.asarray(profile(number_of, total, reach, lean), jnp.int32)
    twos = (number_of - 1) // 2
    giver, taker = lengths[1:1 + 2 * twos:2], lengths[2:2 + 2 * twos:2]
    margin = jnp.minimum(giver - 1, reach - taker)
    passed = jax.random.randint(jax.random.fold_in(rng, 1), (twos,), 0, 1 << 20) % (margin + 1)
    lengths = lengths.at[1:1 + 2 * twos:2].set(giver - passed).at[2:2 + 2 * twos:2].set(taker + passed)
    return lengths[jax.random.permutation(jax.random.fold_in(rng, 2), number_of)]


def shared_out(key, own, number, rows, amount, top, limit, slope):
    ranking = jax.random.permutation(key, amount)
    heavy_load, ordinary = shares(amount, rows * top, limit, slope, True), shares(amount, rows * top, limit, slope, False)
    places = jnp.arange(amount)

    def named(sizes, rotation):
        used = int((sizes > 0).sum())
        fixed = max(1, used // 4)
        passed = fixed + (places - fixed + rotation * (used - fixed)) % max(1, amount - fixed)
        return jnp.zeros((amount,), jnp.int32).at[ranking[jnp.where(places < fixed, places, passed)]].set(jnp.asarray(sizes, jnp.int32))

    sizes = jnp.where(number % 4 == 0, named(heavy_load, number // 4), named(ordinary, number - number // 4 - 1))
    mixed = jax.random.permutation(jax.random.fold_in(own, 3), amount)
    donor, taker = mixed[0:amount // 2 * 2:2], mixed[1:amount // 2 * 2:2]
    room = jnp.minimum(sizes[donor] - 1, limit - sizes[taker]) // 2
    room = jnp.where((donor == ranking[0]) | (taker == ranking[0]) | (sizes[taker] == 0), 0, jnp.maximum(room, 0))
    passed = jax.random.randint(jax.random.fold_in(own, 4), (amount // 2,), 0, 1 << 20) % (room + 1)
    sizes = sizes.at[donor].add(-passed).at[taker].add(passed)
    items = jnp.searchsorted(jnp.cumsum(sizes), jnp.arange(rows * top), side="right").astype(jnp.int32)
    grid = items.reshape(top, rows).T
    grid = grid[jax.random.permutation(jax.random.fold_in(own, 1), rows)]
    rotation = jax.random.randint(jax.random.fold_in(own, 2), (rows, 1), 0, top)
    return jnp.take_along_axis(grid, (jnp.arange(top)[None, :] + rotation) % top, axis=1)


def shares(number_of, total, limit, slope, full):
    loads = [(1 << 20) // math.isqrt(standing ** slope) + 1 for standing in range(1, number_of + 1)]
    largest = limit if full else min(limit, max(-(-total // number_of), total * loads[0] // sum(loads)))
    least = 1 if total - largest >= number_of - 1 else 0
    holding, spare = [largest] + [least] * (number_of - 1), total - largest - least * (number_of - 1)
    while spare > 0:
        candidates = [i for i in range(1, number_of) if holding[i] < largest] or [i for i in range(1, number_of) if holding[i] < limit]
        whole, left = sum([loads[i] for i in candidates]), spare
        for i in candidates:
            addition = min(limit - holding[i], max(1, left * loads[i] // whole), spare)
            holding[i] = holding[i] + addition
            spare = spare - addition
    return np.array(holding)


def centred(own_key, extent, scale, bound, pieces=(), held_as=jnp.bfloat16):
    array = scale * jax.random.normal(own_key, extent, jnp.float32)
    if pieces:
        array = array * levels(own_key, extent, pieces, -0.22, 0.18)
    return jnp.clip(array, -bound, bound).astype(held_as)


def setup_inputs(seed: int = 0) -> dict:
    key_of = jax.random.split(jax.random.key(seed), 12)
    stash = centred(key_of[0], (LAYER_COUNT, TOKENS, MODEL_WIDTH), 1.0, 6.0, ((0, 8), (1, 2), (2, 16)))
    cotangent = centred(key_of[1], (LAYER_COUNT, TOKENS, MODEL_WIDTH), 1.0, 6.0, ((0, 8), (1, 2), (2, 16)))
    backward_expert_routes_keys = jax.random.split(jax.random.fold_in(key_of[2], 1), LAYER_COUNT * TOKENS // TOK_DEV)
    backward_expert_routes_turns = jax.random.permutation(jax.random.fold_in(key_of[2], 3), LAYER_COUNT * TOKENS // TOK_DEV)
    backward_expert_routes = jax.vmap(lambda own, number: shared_out(jax.random.fold_in(key_of[2], 2), own, number, TOK_DEV, EXPERTS, TOP, CAP, 2))(backward_expert_routes_keys, backward_expert_routes_turns).reshape((LAYER_COUNT, TOKENS, TOP))
    backward_job_lengths = jax.vmap(lambda own: uneven(own, ADAPTER_JOBS, TOKENS, TOKENS // 2, 2))(jax.random.split(key_of[3], LAYER_COUNT)).reshape((LAYER_COUNT, ADAPTER_JOBS)).astype(jnp.int32)
    layer_norm_gains = jnp.clip(1.0 + 0.15 * jax.random.normal(key_of[4], (LAYER_COUNT, MODEL_WIDTH), jnp.float32), 0.25, 1.75)
    router = centred(key_of[5], (LAYER_COUNT, MODEL_WIDTH, EXPERTS), MODEL_WIDTH ** -0.5, 0.125, ((0, 8),))
    expert_gate_weight = centred(key_of[6], (LAYER_COUNT, MODEL_WIDTH, EXPERTS * FF), MODEL_WIDTH ** -0.5, 0.125, ((0, 8), (2, 32)))
    expert_up_weight = centred(key_of[7], (LAYER_COUNT, MODEL_WIDTH, EXPERTS * FF), MODEL_WIDTH ** -0.5, 0.125, ((0, 8), (2, 32)))
    expert_down_weight = centred(key_of[8], (LAYER_COUNT, EXPERTS * FF, MODEL_WIDTH), FF ** -0.5, 0.0625, ((0, 8), (1, 32)))
    adapter_down_maps = centred(key_of[9], (LAYER_COUNT, MODEL_WIDTH, ADAPTER_JOBS * ADAPTER_RANK), MODEL_WIDTH ** -0.5, 0.125, ((0, 8), (1, 16)))
    adapter_up_maps = centred(key_of[10], (LAYER_COUNT, ADAPTER_JOBS * ADAPTER_RANK, MODEL_WIDTH), ADAPTER_RANK ** -0.5, 1.5, ((0, 8), (2, 16)))
    return {"stash": stash, "cotangent": cotangent, "backward_expert_routes": backward_expert_routes, "backward_job_lengths": backward_job_lengths, "layer_norm_gains": layer_norm_gains, "router": router, "expert_gate_weight": expert_gate_weight, "expert_up_weight": expert_up_weight, "expert_down_weight": expert_down_weight, "adapter_down_maps": adapter_down_maps, "adapter_up_maps": adapter_up_maps}


EPS = 1e-05
ADAPTER_SCALE = 0.5
HIGH = lax.Precision.HIGHEST

def job_columns(job_token_lengths, offset, count):
    ends = jnp.cumsum(job_token_lengths, dtype=jnp.int32)
    position = offset + jnp.arange(count, dtype=jnp.int32)
    owner = lax.optimization_barrier(jnp.sum((ends[None, :] <= position[:, None]).astype(jnp.int32), axis=1, dtype=jnp.int32))
    column_owner = jnp.arange(job_token_lengths.shape[0] * ADAPTER_RANK, dtype=jnp.int32) // ADAPTER_RANK
    return (owner[:, None] == column_owner[None, :]).astype(jnp.float32)

def prepare(whole_batch, norm_gain_vector, router, token_routes):
    expert_values = whole_batch.astype(jnp.float32)
    scale = lax.rsqrt(lax.optimization_barrier(jnp.mean(expert_values * expert_values, axis=1, keepdims=True)) + EPS)
    normalized_input = (expert_values * scale * norm_gain_vector[None, :]).astype(jnp.bfloat16)
    logits = jnp.dot(normalized_input, router, preferred_element_type=jnp.float32)
    labels = jnp.arange(router.shape[1], dtype=jnp.int32)
    first = (token_routes[:, 0:1] == labels[None, :]).astype(jnp.float32)
    second = (token_routes[:, 1:2] == labels[None, :]).astype(jnp.float32)
    upper = jax.nn.sigmoid(lax.optimization_barrier(jnp.sum(first * logits, axis=1)) - lax.optimization_barrier(jnp.sum(second * logits, axis=1)))
    table = upper[:, None] * first + (1.0 - upper)[:, None] * second
    return (expert_values, scale, normalized_input, first, second, upper, table)

def router_grad(gate_grad, first, second, upper):
    spread = lax.optimization_barrier(jnp.sum(first * gate_grad, axis=1)) - lax.optimization_barrier(jnp.sum(second * gate_grad, axis=1))
    delta = spread * upper * (1.0 - upper)
    return delta[:, None] * (first - second)

def layer_backward_pass(whole_batch, adapter_gradient_list, norm_gain_vector, router, expert_gate_weight, expert_up_weight, expert_down_weight, adapter_down_maps, adapter_up_maps, token_routes, job_token_lengths):
    expert_values, scale, normalized_input, first, second, upper, table = prepare(whole_batch, norm_gain_vector, router, token_routes)
    grad_values = adapter_gradient_list.astype(jnp.float32)
    job_mask = job_columns(job_token_lengths, 0, expert_values.shape[0])
    low_rank_rows = (jnp.dot(normalized_input, adapter_down_maps, preferred_element_type=jnp.float32) * job_mask).astype(jnp.bfloat16)
    grad_low_rank = (ADAPTER_SCALE * jnp.dot(adapter_gradient_list, adapter_up_maps.T, preferred_element_type=jnp.float32) * job_mask).astype(jnp.bfloat16)
    up_map_gradient = ADAPTER_SCALE * jnp.dot(low_rank_rows.T, adapter_gradient_list, preferred_element_type=jnp.float32)
    down_map_gradient = jnp.dot(normalized_input.T, grad_low_rank, preferred_element_type=jnp.float32)
    grad_normalized = jnp.dot(grad_low_rank, adapter_down_maps.T, preferred_element_type=jnp.float32)
    gate_terms = []
    for expert in range(EXPERTS):
        lower_col = expert * FF
        wg = expert_gate_weight[:, lower_col:lower_col + FF]
        wu = expert_up_weight[:, lower_col:lower_col + FF]
        wd = expert_down_weight[lower_col:lower_col + FF, :]
        gate = jnp.dot(normalized_input, wg, preferred_element_type=jnp.float32)
        up = jnp.dot(normalized_input, wu, preferred_element_type=jnp.float32)
        sig = jax.nn.sigmoid(gate)
        act = gate * sig
        hidden = (act * up).astype(jnp.bfloat16)
        output = jnp.dot(hidden, wd, preferred_element_type=jnp.float32)
        gate_terms.append(lax.optimization_barrier(jnp.sum(grad_values * output, axis=1)))
        back = jnp.dot(adapter_gradient_list, wd.T, preferred_element_type=jnp.float32)
        d_gate = (back * up * sig * (1.0 + gate * (1.0 - sig))).astype(jnp.bfloat16)
        d_up = (back * act).astype(jnp.bfloat16)
        inner = jnp.dot(d_gate, wg.T, preferred_element_type=jnp.float32) + jnp.dot(d_up, wu.T, preferred_element_type=jnp.float32)
        grad_normalized = grad_normalized + table[:, expert:expert + 1] * inner
    gate_grad = jnp.stack(gate_terms, axis=1)
    d_logit = router_grad(gate_grad, first, second, upper)
    grad_normalized = grad_normalized + jnp.dot(d_logit, router.astype(jnp.float32).T, precision=HIGH)
    weighted = grad_normalized * norm_gain_vector[None, :]
    stat = lax.optimization_barrier(jnp.sum(weighted * expert_values, axis=1, keepdims=True))
    layer_result = grad_values + scale * weighted - expert_values * scale * scale * scale * stat / MODEL_WIDTH
    return (layer_result.astype(jnp.bfloat16), down_map_gradient, up_map_gradient)

def reference(stash, cotangent, backward_expert_routes, backward_job_lengths, layer_norm_gains, router, expert_gate_weight, expert_up_weight, expert_down_weight, adapter_down_maps, adapter_up_maps):

    def single_layer_tick(items):
        x_stash, adapter_gradient_list, b_routes, b_lengths, norm_gain_vector, route_w, wg, wu, wd, a_map, b_map = items
        return layer_backward_pass(x_stash, adapter_gradient_list, norm_gain_vector, route_w, wg, wu, wd, a_map, b_map, b_routes, b_lengths)
    backward_outputs, down_map_gradient, up_map_gradient = lax.map(single_layer_tick, (stash, cotangent, backward_expert_routes, backward_job_lengths, layer_norm_gains, router, expert_gate_weight, expert_up_weight, expert_down_weight, adapter_down_maps, adapter_up_maps))
    return (jnp.roll(backward_outputs, -1, axis=0), down_map_gradient, up_map_gradient)
```

```python
import jax
import jax.numpy as jnp
from jax import lax
from jax.experimental import pallas as pl
from jax.experimental.pallas import tpu as pltpu
from jax.sharding import Mesh
from jax.sharding import PartitionSpec as P

MODEL_WIDTH = 2048
EXPERTS = 4
RANK = 16
JOBS = 4
CAP = 80
TOK = 128
COLS = 128
GROUPS = 16
STATS = 48
SEND = 2 * CAP + STATS
BACK = CAP + 16
HIDDEN = 896
EXPERT = ("expert_0", "expert_1")
EXPERT_DP = ("expert_0", "expert_1", "dp")
EPS = 1e-05
ADAPTER_SCALE = 0.5
F32 = jnp.float32
BF16 = jnp.bfloat16


def dot(a, b, ca, cb):
    return lax.dot_general(a, b, (((ca,), (cb,)), ((), ())), preferred_element_type=F32)


def high_low(v):
    high = v.astype(BF16)
    return high, (v - high.astype(F32)).astype(BF16)


def slot_places(routes):
    lanes = lax.broadcasted_iota(jnp.int32, (TOK, 128), 1)
    first, second = routes[:, 0:1], routes[:, 1:2]
    member = ((lanes == first) | (lanes == second)).astype(BF16)
    earlier = (
        lax.broadcasted_iota(jnp.int32, (TOK, TOK), 1)
        < lax.broadcasted_iota(jnp.int32, (TOK, TOK), 0)
    ).astype(BF16)
    rank = dot(earlier, member, 1, 0)
    places = []
    for chosen in (first, second):
        at = jnp.sum(jnp.where(lanes == chosen, rank, 0.0), axis=1, keepdims=True)
        places.append(chosen * 128 + at.astype(jnp.int32))
    return places


def owner_mask(scalars, offset, count):
    token = offset + lax.broadcasted_iota(jnp.int32, (JOBS * RANK, count), 1)
    job = lax.broadcasted_iota(jnp.int32, (JOBS * RANK, count), 0) // RANK
    owner = jnp.zeros((JOBS * RANK, count), jnp.int32)
    end = jnp.int32(0)
    for j in range(JOBS):
        end = end + scalars[2 + j]
        owner = owner + (token >= end).astype(jnp.int32)
    return owner == job


def prepare_kernel(scalars, x_ref, g_ref, routes_ref, gain_ref, router_ref, down_ref, up_ref, out_ref):
    x = x_ref[...]
    g = g_ref[...]
    first, second = slot_places(routes_ref[...])
    for e in range(EXPERTS):
        lanes = e * 128 + lax.broadcasted_iota(jnp.int32, (TOK, 128), 1)
        hit = ((lanes == first) | (lanes == second)).astype(F32)
        pick = hit.T[:CAP].astype(BF16)
        xs = dot(pick, x, 1, 0).astype(BF16)
        gs = dot(pick, g, 1, 0).astype(BF16)
        for k in range(GROUPS // EXPERTS):
            out_ref[e * 4 + k, 0:CAP, :] = xs
            out_ref[e * 4 + k, CAP : 2 * CAP, :] = gs
    xf = x.astype(F32)
    xg = (xf * gain_ref[...]).astype(BF16)
    mask = owner_mask(scalars, scalars[1] * TOK, TOK)
    low = jnp.where(mask, dot(down_ref[...].astype(F32).T.astype(BF16), xg, 1, 1), 0.0)
    dlow = jnp.where(mask, dot(up_ref[...], g, 1, 1), 0.0)
    low16 = low[0:16] + low[16:32] + low[32:48] + low[48:64]
    dlow16 = dlow[0:16] + dlow[16:32] + dlow[32:48] + dlow[48:64]
    wide = jnp.concatenate([router_ref[...].astype(F32), jnp.zeros((COLS, 124), F32)], axis=1)
    logits = dot(wide.T[:8].astype(BF16), xg, 1, 1)
    square = xf * xf
    squares = jnp.sum(square.T, axis=0, keepdims=True)
    row = lax.broadcasted_iota(jnp.int32, (8, TOK), 0)
    small = jnp.where(row == 4, squares, logits)
    high = small.astype(BF16).astype(F32)
    stats = jnp.concatenate([low16, dlow16, high, small - high], axis=0).astype(BF16)
    for k in range(GROUPS):
        out_ref[k, 2 * CAP :, :] = stats


def expert_kernel(own_ref, other_ref, gain_ref, wg_ref, wu_ref, wd_ref, own_out, other_out, x_s, g_s, da_s, db_s):
    for d, ref in enumerate((own_ref, other_ref)):
        rows = slice(d * CAP, (d + 1) * CAP)
        total = jnp.zeros((CAP, 128), F32)
        for c in range(GROUPS):
            v = ref[c, 0:CAP, :].astype(F32)
            total = total + v * v
        scale = lax.rsqrt(jnp.sum(total, axis=1, keepdims=True) / MODEL_WIDTH + EPS)
        for c in range(GROUPS):
            cols = slice(c * 128, (c + 1) * 128)
            x_s[rows, cols] = (ref[c, 0:CAP, :].astype(F32) * scale * gain_ref[:, cols]).astype(BF16)
            g_s[rows, cols] = ref[c, CAP : 2 * CAP, :]
    gate_terms = jnp.zeros((2 * CAP, 128), F32)
    stat_terms = jnp.zeros((2 * CAP, 128), F32)
    for lower in range(0, HIDDEN, 256):
        size = min(256, HIDDEN - lower)
        cols = slice(lower, lower + size)
        a = dot(x_s[...], wg_ref[:, cols], 1, 0)
        b = dot(x_s[...], wu_ref[:, cols], 1, 0)
        back = dot(g_s[...], wd_ref[cols, :], 1, 1)
        sig = jax.nn.sigmoid(a)
        act = a * sig
        da = back * b * sig * (1.0 + a * (1.0 - sig))
        db = back * act
        gate = act * b * back
        stat = da * a + db * b
        for k in range(0, size, 128):
            gate_terms = gate_terms + gate[:, k : k + 128]
            stat_terms = stat_terms + stat[:, k : k + 128]
        da_s[:, cols] = da.astype(BF16)
        db_s[:, cols] = db.astype(BF16)
    lane = lax.broadcasted_iota(jnp.int32, (2 * CAP, 128), 1)
    dgate = jnp.sum(gate_terms, axis=1, keepdims=True)
    dstat = jnp.sum(stat_terms, axis=1, keepdims=True)
    table = jnp.where(lane == 0, dgate, jnp.where(lane == 1, dstat, 0.0))
    row = lax.broadcasted_iota(jnp.int32, (8, 128), 0)
    for d, out in enumerate((own_out, other_out)):
        part = jnp.concatenate([table[d * CAP : (d + 1) * CAP], jnp.zeros((128 - CAP, 128), F32)], axis=0)
        lines = part.T[0:8]
        high = lines.astype(BF16).astype(F32)
        packed = jnp.where(row < 2, high, 0.0) + jnp.where((row >= 2) & (row < 4), jnp.roll(lines - high, 2, 0), 0.0)
        packed = jnp.concatenate([packed, jnp.zeros((8, 128), F32)] if d == 0 else [jnp.zeros((8, 128), F32), packed], axis=0)
        for c in range(GROUPS):
            out[c, CAP:BACK, :] = packed.astype(out.dtype)
    for lower in range(0, MODEL_WIDTH, 256):
        rows = slice(lower, lower + 256)
        dn = dot(da_s[...], wg_ref[rows, :], 1, 1) + dot(db_s[...], wu_ref[rows, :], 1, 1)
        for k in range(2):
            c = lower // 128 + k
            own_out[c, 0:CAP, :] = dn[0:CAP, k * 128 : (k + 1) * 128]
            other_out[c, 0:CAP, :] = dn[CAP:, k * 128 : (k + 1) * 128].astype(BF16)


def stats_kernel(
    scalars, own_ref, other_ref, x_ref, g_ref, xo_ref, go_ref, gain_ref, down_ref,
    grad_down_ref, grad_up_ref, side_ref, base_ref, sb_ref
):
    grad_down = jnp.zeros((JOBS * RANK, COLS), F32)
    grad_up = jnp.zeros((JOBS * RANK, COLS), F32)
    me = scalars[1]
    for d, (ref, xr, gr) in enumerate(((own_ref, x_ref, g_ref), (other_ref, xo_ref, go_ref))):
        total = ref[0, 2 * CAP :, :].astype(F32)
        for c in range(1, GROUPS):
            total = total + ref[c, 2 * CAP :, :].astype(F32)
        small = total[32:40] + total[40:48]
        scale = lax.rsqrt(small[4:5] / MODEL_WIDTH + EPS)
        block = me if d == 0 else 1 - me
        mask = owner_mask(scalars, block * TOK, TOK)
        low16 = total[0:16]
        dlow16 = ADAPTER_SCALE * total[16:32]
        low = jnp.where(mask, jnp.concatenate([low16 * scale] * JOBS, axis=0), 0.0).astype(BF16)
        dlow = jnp.where(mask, jnp.concatenate([dlow16] * JOBS, axis=0), 0.0).astype(BF16)
        row = lax.broadcasted_iota(jnp.int32, (8, TOK), 0)
        adapter_stat = jnp.sum(dlow16.astype(BF16).astype(F32) * low16, axis=0, keepdims=True)
        lines = jnp.where(row == 4, scale, jnp.where(row == 5, adapter_stat, small))
        side = jnp.concatenate([lines, jnp.zeros((120, TOK), F32)], axis=0).T
        xf = xr[...].astype(F32)
        scale_col = side[:, 4:5]
        normed = (xf * scale_col * gain_ref[...]).astype(BF16)
        grad_down = grad_down + dot(dlow, normed, 1, 0)
        grad_up = grad_up + dot(low, gr[...], 1, 0)
        if d == 0:
            side_ref[...] = side
            adapter = dot(down_ref[...], dlow, 1, 0).T
            base_ref[...] = gr[...].astype(F32) + scale_col * adapter * gain_ref[...]
            sb_ref[...] = xf * scale_col * scale_col * scale_col / MODEL_WIDTH
    wide = jnp.concatenate([grad_down, jnp.zeros((64, COLS), F32)], axis=0)
    grad_down_ref[...] = wide.T[:, 0 : JOBS * RANK]
    grad_up_ref[...] = ADAPTER_SCALE * grad_up


def finish_kernel(scalars, in_ref, routes_ref, gain_ref, router_ref, side_ref, base_ref, sb_ref, out_ref):
    routes = routes_ref[...]
    first, second = slot_places(routes)
    side = side_ref[...]
    lane = lax.broadcasted_iota(jnp.int32, (TOK, 128), 1)

    def chosen(k):
        return jnp.sum(jnp.where(lane == routes[:, k : k + 1], side, 0.0), axis=1, keepdims=True)

    scale = side[:, 4:5]
    raw = chosen(0) - chosen(1)
    upper = jax.nn.sigmoid(raw * scale)
    lower = 1.0 - upper
    rows1 = jnp.zeros((TOK, COLS), F32)
    rows2 = jnp.zeros((TOK, COLS), F32)
    gate1 = jnp.zeros((TOK, 128), F32)
    gate2 = jnp.zeros((TOK, 128), F32)
    stat1 = jnp.zeros((TOK, 128), F32)
    stat2 = jnp.zeros((TOK, 128), F32)
    for e in range(EXPERTS):
        total = in_ref[4 * e].astype(F32)
        for k in range(1, 4):
            total = total + in_ref[4 * e + k].astype(F32)
        lines = total[CAP : CAP + 8] + total[CAP + 8 : CAP + 16]
        dgate = lines[0:1] + lines[2:3]
        dstat = lines[1:2] + lines[3:4]
        hit1 = lane + e * 128 == first
        hit2 = lane + e * 128 == second
        gate1 = gate1 + jnp.where(hit1, dgate, 0.0)
        gate2 = gate2 + jnp.where(hit2, dgate, 0.0)
        stat1 = stat1 + jnp.where(hit1, dstat, 0.0)
        stat2 = stat2 + jnp.where(hit2, dstat, 0.0)
        high, low = high_low(total[0:CAP])
        one = hit1[:, 0:CAP].astype(BF16)
        two = hit2[:, 0:CAP].astype(BF16)
        rows1 = rows1 + dot(one, high, 1, 0) + dot(one, low, 1, 0)
        rows2 = rows2 + dot(two, high, 1, 0) + dot(two, low, 1, 0)
    spread = jnp.sum(gate1 - gate2, axis=1, keepdims=True)
    delta = spread * upper * lower
    expert_stat = upper * jnp.sum(stat1, axis=1, keepdims=True) + lower * jnp.sum(stat2, axis=1, keepdims=True)
    stat = expert_stat / scale + side[:, 5:6] + delta * raw
    wide = jnp.concatenate([router_ref[...].astype(F32), jnp.zeros((COLS, 124), F32)], axis=1).T
    routed = jnp.zeros((TOK, COLS), F32)
    for e in range(EXPERTS):
        sign = (routes[:, 0:1] == e).astype(F32) - (routes[:, 1:2] == e).astype(F32)
        routed = routed + sign * wide[e : e + 1]
    dnormed = upper * rows1 + lower * rows2 + delta * routed
    result = base_ref[...] + scale * dnormed * gain_ref[...] - sb_ref[...] * stat
    out_ref[...] = result.astype(BF16)


def whole(shape):
    return pl.BlockSpec(shape, lambda i, s: (0,) * len(shape))


GAIN_BLOCK = pl.BlockSpec((1, COLS), lambda i, s: (0, s[0]))
ROUTER_BLOCK = pl.BlockSpec((COLS, EXPERTS), lambda i, s: (s[0], 0))


def call(kernel, scalars, in_specs, out_specs, out_shape, args, scratch=()):
    return pl.pallas_call(
        kernel,
        grid_spec=pltpu.PrefetchScalarGridSpec(
            num_scalar_prefetch=1, grid=(1,), in_specs=in_specs, out_specs=out_specs, scratch_shapes=scratch
        ),
        out_shape=out_shape,
    )(scalars, *args)


def shards(stash, cotangent, routes, lengths, gains, router, wg, wu, wd, down, up):
    x, g, routes, router = stash[0], cotangent[0], routes[0], router[0]
    wg, wu, wd, down, up = wg[0], wu[0], wd[0], down[0], up[0]
    shape = jax.ShapeDtypeStruct
    scalars = jnp.concatenate(
        [
            jnp.stack([lax.axis_index(EXPERT), lax.axis_index("dp")]).astype(jnp.int32),
            lengths[0],
        ]
    )
    swap = [(0, 1), (1, 0)]
    xo = lax.ppermute(x, "dp", swap)
    go = lax.ppermute(g, "dp", swap)
    sent = call(
        prepare_kernel,
        scalars,
        [
            whole((TOK, COLS)), whole((TOK, COLS)), whole((TOK, 2)), GAIN_BLOCK, ROUTER_BLOCK,
            whole((COLS, JOBS * RANK)), whole((JOBS * RANK, COLS)),
        ],
        whole((GROUPS, SEND, 128)),
        shape((GROUPS, SEND, 128), BF16),
        (x, g, routes, gains, router, down, up),
    )
    own = lax.all_to_all(sent, EXPERT, 0, 0, tiled=True)
    other = lax.ppermute(own, "dp", swap)
    vmem = pl.BlockSpec(memory_space=pltpu.VMEM)
    own_part, other_part = pl.pallas_call(
        expert_kernel,
        in_specs=[vmem] * 6,
        out_specs=(vmem, vmem),
        out_shape=(shape((GROUPS, BACK, 128), F32), shape((GROUPS, BACK, 128), BF16)),
        scratch_shapes=[
            pltpu.VMEM((2 * CAP, MODEL_WIDTH), BF16),
            pltpu.VMEM((2 * CAP, MODEL_WIDTH), BF16),
            pltpu.VMEM((2 * CAP, HIDDEN), BF16),
            pltpu.VMEM((2 * CAP, HIDDEN), BF16),
        ],
        compiler_params=pltpu.CompilerParams(vmem_limit_bytes=40 * 1024 * 1024),
    )(own, other, gains, wg, wu, wd)
    arrived = lax.ppermute(other_part, "dp", swap)
    parts = (own_part + arrived.astype(F32)).astype(BF16)
    back = lax.all_to_all(parts, EXPERT, 0, 0, tiled=True)
    grad_down, grad_up, side, base, sb = call(
        stats_kernel,
        scalars,
        [
            whole((GROUPS, SEND, 128)), whole((GROUPS, SEND, 128)), whole((TOK, COLS)), whole((TOK, COLS)),
            whole((TOK, COLS)), whole((TOK, COLS)), GAIN_BLOCK, whole((COLS, JOBS * RANK)),
        ],
        (whole((COLS, JOBS * RANK)), whole((JOBS * RANK, COLS)), whole((TOK, 128)), whole((TOK, COLS)), whole((TOK, COLS))),
        (
            shape((COLS, JOBS * RANK), F32), shape((JOBS * RANK, COLS), F32), shape((TOK, 128), F32),
            shape((TOK, COLS), F32), shape((TOK, COLS), F32),
        ),
        (own, other, x, g, xo, go, gains, down),
    )
    result = call(
        finish_kernel,
        scalars,
        [
            whole((GROUPS, BACK, 128)), whole((TOK, 2)), GAIN_BLOCK, ROUTER_BLOCK,
            whole((TOK, 128)), whole((TOK, COLS)), whole((TOK, COLS)),
        ],
        whole((TOK, COLS)),
        shape((TOK, COLS), BF16),
        (back, routes, gains, router, side, base, sb),
    )
    count = lax.axis_size("section")
    handed = lax.ppermute(result, "section", [(i, (i - 1) % count) for i in range(count)])
    return handed[None], grad_down[None], grad_up[None]


def solution(mesh):
    finer = Mesh(
        mesh.devices.reshape(mesh.shape["section"], 4, 4, mesh.shape["dp"]),
        ("section", "expert_0", "expert_1", "dp"),
    )
    in_specs = (
        P("section", "dp", EXPERT),
        P("section", "dp", EXPERT),
        P("section", "dp", None),
        P("section", None),
        P("section", None),
        P("section", None, None),
        P("section", None, EXPERT_DP),
        P("section", None, EXPERT_DP),
        P("section", EXPERT_DP, None),
        P("section", EXPERT, None),
        P("section", None, EXPERT),
    )
    out_specs = (P("section", "dp", EXPERT), P("section", EXPERT, None), P("section", None, EXPERT))
    return jax.shard_map(shards, mesh=finer, in_specs=in_specs, out_specs=out_specs, check_vma=False)
```

```python
import jax
import jax.numpy as jnp
from jax import lax
from jax.experimental import pallas as pl
from jax.experimental.pallas import tpu as pltpu
from jax.sharding import Mesh
from jax.sharding import PartitionSpec as P

MODEL_WIDTH = 2048
EXPERTS = 4
RANK = 16
JOBS = 4
CAP = 80
TOK = 128
COLS = 128
GROUPS = 16
STATS = 48
SEND = 2 * CAP + STATS
BACK = CAP + 16
HIDDEN = 896
EXPERT = ("expert_0", "expert_1")
EXCHANGE = ("expert_1", "expert_0")
EXPERT_DP = ("expert_0", "expert_1", "dp")
EPS = 1e-05
ADAPTER_SCALE = 0.5
F32 = jnp.float32
BF16 = jnp.bfloat16


def dot(a, b, ca, cb):
    return lax.dot_general(a, b, (((ca,), (cb,)), ((), ())), preferred_element_type=F32)


def stand(c):
    return c % 4 * 4 + c // 4


def high_low(v):
    high = v.astype(BF16)
    return high, (v - high.astype(F32)).astype(BF16)


def members(routes):
    label = lax.broadcasted_iota(jnp.int32, (8, TOK), 0)
    member = (label == routes[0:1]) | (label == routes[1:2])
    earlier = (
        lax.broadcasted_iota(jnp.int32, (TOK, TOK), 0)
        < lax.broadcasted_iota(jnp.int32, (TOK, TOK), 1)
    ).astype(BF16)
    rank = dot(member.astype(BF16), earlier, 1, 0)
    return label, member, rank


def owner_mask(lengths, offset, count):
    token = offset + lax.broadcasted_iota(jnp.int32, (JOBS * RANK, count), 1)
    job = lax.broadcasted_iota(jnp.int32, (JOBS * RANK, count), 0) // RANK
    owner = jnp.zeros((JOBS * RANK, count), jnp.int32)
    end = jnp.int32(0)
    for j in range(JOBS):
        end = end + lengths[0, j]
        owner = owner + (token >= end).astype(jnp.int32)
    return owner == job


def local_columns(ref, column):
    return ref[:, pl.ds(pl.multiple_of(column * COLS, COLS), COLS)]


def prepare_kernel(column, block, *refs):
    sources, out_ref, sem = refs[:8], refs[8], refs[17]
    lengths, x_ref, g_ref, routes_ref, gain_ref, router_ref, down_ref, up_ref = refs[9:17]
    copies = [pltpu.make_async_copy(a, b, sem.at[i]) for i, (a, b) in enumerate(zip(sources, refs[9:17]))]
    for copy in copies:
        copy.start()
    for copy in copies:
        copy.wait()
    x = x_ref[...]
    g = g_ref[...]
    _, member, rank = members(routes_ref[...])
    slot = lax.broadcasted_iota(jnp.int32, (CAP, TOK), 0)
    place = jnp.where(member, rank.astype(jnp.int32), -1)
    for e in range(EXPERTS):
        pick = (place[e : e + 1] == slot).astype(BF16)
        xs = dot(pick, x, 1, 0).astype(BF16)
        gs = dot(pick, g, 1, 0).astype(BF16)
        for k in range(GROUPS // EXPERTS):
            out_ref[stand(e * 4 + k), 0:CAP, :] = xs
            out_ref[stand(e * 4 + k), CAP : 2 * CAP, :] = gs
    xf = x.astype(F32)
    xg = (xf * local_columns(gain_ref, column[0])).astype(BF16)
    mask = owner_mask(lengths, block[0] * TOK, TOK)
    low = jnp.where(mask, dot(down_ref[...], xg, 1, 1), 0.0)
    dlow = jnp.where(mask, dot(up_ref[...], g, 1, 1), 0.0)
    low16 = low[0:16] + low[16:32] + low[32:48] + low[48:64]
    dlow16 = dlow[0:16] + dlow[16:32] + dlow[32:48] + dlow[48:64]
    router = local_columns(router_ref, column[0]).astype(F32)
    wide = jnp.concatenate([router, jnp.zeros((4, COLS), F32)], axis=0)
    logits = dot(wide.astype(BF16), xg, 1, 1)
    square = xf * xf
    squares = jnp.sum(square.T, axis=0, keepdims=True)
    row = lax.broadcasted_iota(jnp.int32, (8, TOK), 0)
    small = jnp.where(row == 4, squares, logits)
    high = small.astype(BF16).astype(F32)
    stats = jnp.concatenate([low16, dlow16, high, small - high], axis=0).astype(BF16)
    for k in range(GROUPS):
        out_ref[k, 2 * CAP :, :] = stats


def weights_kernel(gain_ref, *refs):
    sources, gain_out, targets, sem, gain_sem = refs[:3], refs[3], refs[4:7], refs[7], refs[8]
    copies = [pltpu.make_async_copy(gain_ref, gain_out, gain_sem)]
    for i, (source, target) in enumerate(zip(sources, targets)):
        size = source.shape[0] // 4
        for k in range(4):
            rows = slice(k * size, (k + 1) * size)
            copies.append(pltpu.make_async_copy(source.at[rows], target.at[rows], sem.at[i, k]))
    for copy in copies:
        copy.start()
    for copy in copies:
        copy.wait()


CHUNKS = tuple((at, min(256, HIDDEN - at)) for at in range(0, HIDDEN, 256))


def expert_kernel(own_ref, other_ref, gain_ref, wg_ref, wu_ref, wd_ref, own_out, other_out, x_s, g_s, da_s, db_s):
    for d, ref in enumerate((own_ref, other_ref)):
        rows = slice(d * CAP, (d + 1) * CAP)
        total = jnp.zeros((CAP, 128), F32)
        for c in range(GROUPS):
            v = ref[c, 0:CAP, :].astype(F32)
            total = total + v * v
        scale = lax.rsqrt(jnp.sum(total, axis=1, keepdims=True) / MODEL_WIDTH + EPS)
        for c in range(GROUPS):
            cols = slice(c * 128, (c + 1) * 128)
            x_s[rows, cols] = (ref[stand(c), 0:CAP, :].astype(F32) * scale * gain_ref[:, cols]).astype(BF16)
            g_s[rows, cols] = ref[stand(c), CAP : 2 * CAP, :]
    gate_terms = jnp.zeros((2 * CAP, 128), F32)
    stat_terms = jnp.zeros((2 * CAP, 128), F32)
    for lower, size in CHUNKS:
        cols = slice(lower, lower + size)
        a = dot(x_s[...], wg_ref[:, cols], 1, 0)
        b = dot(x_s[...], wu_ref[:, cols], 1, 0)
        back = dot(g_s[...], wd_ref[cols, :], 1, 1)
        sig = jax.nn.sigmoid(a)
        act = a * sig
        da = back * b * sig * (1.0 + a * (1.0 - sig))
        db = back * act
        gate = act * b * back
        stat = da * a + db * b
        for k in range(0, size, 128):
            gate_terms = gate_terms + gate[:, k : k + 128]
            stat_terms = stat_terms + stat[:, k : k + 128]
        da_s[:, cols] = da.astype(BF16)
        db_s[:, cols] = db.astype(BF16)
    lane = lax.broadcasted_iota(jnp.int32, (2 * CAP, 128), 1)
    dgate = jnp.sum(gate_terms, axis=1, keepdims=True)
    dstat = jnp.sum(stat_terms, axis=1, keepdims=True)
    table = jnp.where(lane == 0, dgate, jnp.where(lane == 1, dstat, 0.0))
    row = lax.broadcasted_iota(jnp.int32, (8, 128), 0)
    for d, out in enumerate((own_out, other_out)):
        part = jnp.concatenate([table[d * CAP : (d + 1) * CAP], jnp.zeros((128 - CAP, 128), F32)], axis=0)
        lines = part.T[0:8]
        high = lines.astype(BF16).astype(F32)
        packed = jnp.where(row < 2, high, 0.0) + jnp.where((row >= 2) & (row < 4), jnp.roll(lines - high, 2, 0), 0.0)
        packed = jnp.concatenate([packed, jnp.zeros((8, 128), F32)] if d == 0 else [jnp.zeros((8, 128), F32), packed], axis=0)
        for c in range(GROUPS):
            out[c, CAP:BACK, :] = packed.astype(out.dtype)
    for lower in range(0, MODEL_WIDTH, 256):
        rows = slice(lower, lower + 256)
        dn = dot(da_s[...], wg_ref[rows, :], 1, 1) + dot(db_s[...], wu_ref[rows, :], 1, 1)
        for k in range(2):
            c = lower // 128 + k
            own_out[stand(c), 0:CAP, :] = dn[0:CAP, k * 128 : (k + 1) * 128]
            other_out[stand(c), 0:CAP, :] = dn[CAP:, k * 128 : (k + 1) * 128].astype(BF16)


def stats_kernel(
    column, block, lengths, own_ref, other_ref, x_ref, g_ref, xo_ref, go_ref, routes_ref, gain_ref, down_ref, router_ref,
    grad_down_ref, grad_up_ref, side_ref, base_ref, sb_ref, take_ref, hits_ref, routed_ref,
):
    grad_down = jnp.zeros((JOBS * RANK, COLS), F32)
    grad_up = jnp.zeros((JOBS * RANK, COLS), F32)
    gain = local_columns(gain_ref, column[0])
    row = lax.broadcasted_iota(jnp.int32, (8, TOK), 0)
    for d, (ref, xr, gr) in enumerate(((own_ref, x_ref, g_ref), (other_ref, xo_ref, go_ref))):
        total = ref[0, 2 * CAP :, :].astype(F32)
        for c in range(1, GROUPS):
            total = total + ref[c, 2 * CAP :, :].astype(F32)
        small = total[32:40] + total[40:48]
        scale = lax.rsqrt(small[4:5] / MODEL_WIDTH + EPS)
        mask = owner_mask(lengths, (block[0] if d == 0 else 1 - block[0]) * TOK, TOK)
        low16 = total[0:16]
        dlow16 = ADAPTER_SCALE * total[16:32]
        low = jnp.where(mask, jnp.concatenate([low16 * scale] * JOBS, axis=0), 0.0).astype(BF16)
        dlow = jnp.where(mask, jnp.concatenate([dlow16] * JOBS, axis=0), 0.0).astype(BF16)
        if d == 0:
            routes = routes_ref[...]
            label, member, rank = members(routes)
            first = label == routes[0:1]
            second = label == routes[1:2]
            raw = jnp.sum(jnp.where(first, small, 0.0) - jnp.where(second, small, 0.0), axis=0, keepdims=True)
            upper = jax.nn.sigmoid(raw * scale)
            adapter_stat = jnp.sum(dlow16.astype(BF16).astype(F32) * low16, axis=0, keepdims=True)
            at1 = jnp.sum(jnp.where(first, rank, 0.0), axis=0, keepdims=True)
            at2 = jnp.sum(jnp.where(second, rank, 0.0), axis=0, keepdims=True)
            lines = [scale, adapter_stat, raw, upper, at1, at2, routes[0:1].astype(F32), routes[1:2].astype(F32)]
        else:
            lines = [scale] * 8
        packed = jnp.zeros((8, TOK), F32)
        for k, line in enumerate(lines):
            packed = jnp.where(row == k, line, packed)
        side = jnp.concatenate([packed, jnp.zeros((120, TOK), F32)], axis=0).T
        scale_col = side[:, 0:1]
        xf = xr[...].astype(F32)
        normed = (xf * scale_col * gain).astype(BF16)
        grad_down = grad_down + dot(dlow, normed, 1, 0)
        grad_up = grad_up + dot(low, gr[...], 1, 0)
        if d == 0:
            side_ref[...] = side
            wide = jnp.concatenate([down_ref[...].astype(F32), jnp.zeros((64, COLS), F32)], axis=0)
            adapter = dot(wide.T.astype(BF16)[:, 0 : JOBS * RANK], dlow, 1, 0).T
            base_ref[...] = gr[...].astype(F32) + scale_col * adapter * gain
            sb_ref[...] = xf * scale_col * scale_col * scale_col / MODEL_WIDTH
            lane = lax.broadcasted_iota(jnp.int32, (TOK, 128), 1)
            upper = side[:, 3:4]
            at1, at2 = side[:, 4:5].astype(jnp.int32), side[:, 5:6].astype(jnp.int32)
            first, second = side[:, 6:7].astype(jnp.int32), side[:, 7:8].astype(jnp.int32)
            router = local_columns(router_ref, column[0]).astype(F32)
            routed = jnp.zeros((TOK, COLS), F32)
            for e in range(EXPERTS):
                hit1 = ((lane == at1) & (first == e)).astype(F32)
                hit2 = ((lane == at2) & (second == e)).astype(F32)
                take = upper * hit1 + (1.0 - upper) * hit2
                high = take.astype(BF16)
                take_ref[0, e] = high
                take_ref[1, e] = (take - high.astype(F32)).astype(BF16)
                hits_ref[0, e] = take
                hits_ref[1, e] = hit1 - hit2
                sign = (first == e).astype(F32) - (second == e).astype(F32)
                routed = routed + sign * router[e : e + 1]
            routed_ref[...] = routed
    grad_down_ref[...] = grad_down
    grad_up_ref[...] = ADAPTER_SCALE * grad_up


def finish_kernel(column, in_ref, gain_ref, side_ref, base_ref, sb_ref, take_ref, hits_ref, routed_ref, out_ref):
    side = side_ref[...]
    scale, adapter_stat, raw, upper = (side[:, k : k + 1] for k in range(4))
    rows = jnp.zeros((TOK, COLS), F32)
    spread = jnp.zeros((TOK, 128), F32)
    stat = jnp.zeros((TOK, 128), F32)
    for e in range(EXPERTS):
        total = in_ref[stand(4 * e)].astype(F32)
        for k in range(1, 4):
            total = total + in_ref[stand(4 * e + k)].astype(F32)
        lines = total[CAP : CAP + 8] + total[CAP + 8 : CAP + 16]
        spread = spread + hits_ref[1, e] * (lines[0:1] + lines[2:3])
        stat = stat + hits_ref[0, e] * (lines[1:2] + lines[3:4])
        high, low = high_low(total[0:CAP])
        take = take_ref[0, e, :, 0:CAP]
        rows = rows + dot(take, high, 1, 0) + dot(take, low, 1, 0) + dot(take_ref[1, e, :, 0:CAP], high, 1, 0)
    delta = jnp.sum(spread, axis=1, keepdims=True) * upper * (1.0 - upper)
    stat = jnp.sum(stat, axis=1, keepdims=True) / scale + adapter_stat + delta * raw
    dnormed = rows + delta * routed_ref[...]
    result = base_ref[...] + scale * dnormed * local_columns(gain_ref, column[0]) - sb_ref[...] * stat
    out_ref[...] = result.astype(BF16)


VMEM = pl.BlockSpec(memory_space=pltpu.VMEM)
SMEM = pl.BlockSpec(memory_space=pltpu.SMEM)
HBM = pl.BlockSpec(memory_space=pltpu.HBM)


def pinned(v):
    return pltpu.with_memory_space_constraint(v, pltpu.HBM)


def call(kernel, out_shape, scalars, args, scratch=(), arg_specs=None):
    return pl.pallas_call(
        kernel,
        in_specs=[SMEM] * len(scalars) + (arg_specs or [VMEM] * len(args)),
        out_specs=VMEM if isinstance(out_shape, jax.ShapeDtypeStruct) else (VMEM,) * len(out_shape),
        out_shape=out_shape,
        scratch_shapes=scratch,
        compiler_params=pltpu.CompilerParams(vmem_limit_bytes=32 * 1024 * 1024),
    )(*scalars, *(pinned(v) if spec is HBM else v for v, spec in zip(args, arg_specs or [VMEM] * len(args))))


def shards(stash, cotangent, routes, lengths, gains, router, wg, wu, wd, down, up):
    x, g = stash[0], cotangent[0]
    routes, router, down = routes[0].T, router[0].T, down[0].T
    wg, wu, wd, up = wg[0], wu[0], wd[0], up[0]
    shape = jax.ShapeDtypeStruct
    column = lax.axis_index(EXPERT).astype(jnp.int32).reshape(1)
    block = lax.axis_index("dp").astype(jnp.int32).reshape(1)
    swap = [(0, 1), (1, 0)]
    xo = lax.ppermute(x, "dp", swap)
    go = lax.ppermute(g, "dp", swap)
    locals_ = (lengths, x, g, routes, gains, router, down, up)
    sent = call(
        prepare_kernel,
        shape((GROUPS, SEND, 128), BF16),
        (column, block),
        locals_,
        [pltpu.SMEM(lengths.shape, jnp.int32)]
        + [pltpu.VMEM(v.shape, v.dtype) for v in locals_[1:]]
        + [pltpu.SemaphoreType.DMA((8,))],
        [HBM] * 8,
    )
    own = lax.all_to_all(sent, EXCHANGE, 0, 0, tiled=True)
    other = lax.ppermute(own, "dp", swap)
    gains_here, *weights = call(
        weights_kernel,
        tuple(shape(v.shape, v.dtype) for v in (gains, wg, wu, wd)),
        (),
        (gains, wg, wu, wd),
        [pltpu.SemaphoreType.DMA((3, 4)), pltpu.SemaphoreType.DMA],
        [HBM] * 4,
    )
    own_part, other_part = call(
        expert_kernel,
        (shape((GROUPS, BACK, 128), F32), shape((GROUPS, BACK, 128), BF16)),
        (),
        (own, other, gains_here, *weights),
        [
            pltpu.VMEM((2 * CAP, MODEL_WIDTH), BF16),
            pltpu.VMEM((2 * CAP, MODEL_WIDTH), BF16),
            pltpu.VMEM((2 * CAP, HIDDEN), BF16),
            pltpu.VMEM((2 * CAP, HIDDEN), BF16),
        ],
    )
    arrived = lax.ppermute(other_part, "dp", swap)
    parts = (own_part + arrived.astype(F32)).astype(BF16)
    back = lax.all_to_all(parts, EXCHANGE, 0, 0, tiled=True)
    small = shape((JOBS * RANK, COLS), F32)
    square = shape((TOK, COLS), F32)
    grad_down, grad_up, side, base, sb, take, hits, routed = call(
        stats_kernel,
        (
            small, small, square, square, square,
            shape((2, EXPERTS, TOK, 128), BF16), shape((2, EXPERTS, TOK, 128), F32), square,
        ),
        (column, block, lengths),
        (own, other, x, g, xo, go, routes, gains, down, router),
    )
    result = call(
        finish_kernel,
        shape((TOK, COLS), BF16),
        (column,),
        (back, gains, side, base, sb, take, hits, routed),
    )
    count = lax.axis_size("section")
    handed = lax.ppermute(result, "section", [(i, (i - 1) % count) for i in range(count)])
    return handed[None], grad_down.T[None], grad_up[None]


def solution(mesh):
    finer = Mesh(
        mesh.devices.reshape(mesh.shape["section"], 4, 4, mesh.shape["dp"]),
        ("section", "expert_0", "expert_1", "dp"),
    )
    in_specs = (
        P("section", "dp", EXPERT),
        P("section", "dp", EXPERT),
        P("section", "dp", None),
        P("section", None),
        P("section", None),
        P("section", None, None),
        P("section", None, EXPERT_DP),
        P("section", None, EXPERT_DP),
        P("section", EXPERT_DP, None),
        P("section", EXPERT, None),
        P("section", None, EXPERT),
    )
    out_specs = (P("section", "dp", EXPERT), P("section", EXPERT, None), P("section", None, EXPERT))
    return jax.shard_map(shards, mesh=finer, in_specs=in_specs, out_specs=out_specs, check_vma=False)
```

```python
import jax
import jax.numpy as jnp
from jax import lax
from jax.experimental import pallas as pl
from jax.experimental.pallas import tpu as pltpu
from jax.sharding import Mesh
from jax.sharding import PartitionSpec as P

MODEL_WIDTH = 2048
EXPERTS = 4
RANK = 16
JOBS = 4
CAP = 80
TOK = 128
COLS = 128
GROUPS = 16
STATS = 48
SEND = 2 * CAP + STATS
BACK = CAP + 16
HIDDEN = 896
EARLY = 256
EXPERT = ("expert_0", "expert_1")
EXCHANGE = ("expert_1", "expert_0")
EXPERT_DP = ("expert_0", "expert_1", "dp")
EPS = 1e-05
ADAPTER_SCALE = 0.5
F32 = jnp.float32
BF16 = jnp.bfloat16


def dot(a, b, ca, cb):
    return lax.dot_general(a, b, (((ca,), (cb,)), ((), ())), preferred_element_type=F32)


def stand(c):
    return c % 4 * 4 + c // 4


def high_low(v):
    high = v.astype(BF16)
    return high, (v - high.astype(F32)).astype(BF16)


def members(routes):
    label = lax.broadcasted_iota(jnp.int32, (8, TOK), 0)
    member = (label == routes[0:1]) | (label == routes[1:2])
    earlier = (
        lax.broadcasted_iota(jnp.int32, (TOK, TOK), 0)
        < lax.broadcasted_iota(jnp.int32, (TOK, TOK), 1)
    ).astype(BF16)
    rank = dot(member.astype(BF16), earlier, 1, 0)
    return label, member, rank


def owner_mask(lengths, offset, count):
    token = offset + lax.broadcasted_iota(jnp.int32, (JOBS * RANK, count), 1)
    job = lax.broadcasted_iota(jnp.int32, (JOBS * RANK, count), 0) // RANK
    owner = jnp.zeros((JOBS * RANK, count), jnp.int32)
    end = jnp.int32(0)
    for j in range(JOBS):
        end = end + lengths[0, j]
        owner = owner + (token >= end).astype(jnp.int32)
    return owner == job


def local_columns(ref, column):
    return ref[:, pl.ds(pl.multiple_of(column * COLS, COLS), COLS)]


def prepare_kernel(column, block, *refs):
    sources, wd_hbm, out_ref, early_ref, sem = refs[:8], refs[8], refs[9], refs[10], refs[19]
    lengths, x_ref, g_ref, routes_ref, gain_ref, router_ref, down_ref, up_ref = refs[11:19]
    copies = [pltpu.make_async_copy(a, b, sem.at[i]) for i, (a, b) in enumerate(zip(sources, refs[11:19]))]
    early = []
    for k in range(EARLY // 128):
        rows = slice(k * 128, (k + 1) * 128)
        early.append(pltpu.make_async_copy(wd_hbm.at[rows], early_ref.at[rows], sem.at[8 + k]))
    for copy in copies:
        copy.start()
    for copy in early:
        copy.start()
    for copy in copies:
        copy.wait()
    x = x_ref[...]
    g = g_ref[...]
    _, member, rank = members(routes_ref[...])
    slot = lax.broadcasted_iota(jnp.int32, (CAP, TOK), 0)
    place = jnp.where(member, rank.astype(jnp.int32), -1)
    for e in range(EXPERTS):
        pick = (place[e : e + 1] == slot).astype(BF16)
        xs = dot(pick, x, 1, 0).astype(BF16)
        gs = dot(pick, g, 1, 0).astype(BF16)
        for k in range(GROUPS // EXPERTS):
            out_ref[stand(e * 4 + k), 0:CAP, :] = xs
            out_ref[stand(e * 4 + k), CAP : 2 * CAP, :] = gs
    xf = x.astype(F32)
    xg = (xf * local_columns(gain_ref, column[0])).astype(BF16)
    mask = owner_mask(lengths, block[0] * TOK, TOK)
    low = jnp.where(mask, dot(down_ref[...], xg, 1, 1), 0.0)
    dlow = jnp.where(mask, dot(up_ref[...], g, 1, 1), 0.0)
    low16 = low[0:16] + low[16:32] + low[32:48] + low[48:64]
    dlow16 = dlow[0:16] + dlow[16:32] + dlow[32:48] + dlow[48:64]
    router = local_columns(router_ref, column[0]).astype(F32)
    wide = jnp.concatenate([router, jnp.zeros((4, COLS), F32)], axis=0)
    logits = dot(wide.astype(BF16), xg, 1, 1)
    square = xf * xf
    squares = jnp.sum(square.T, axis=0, keepdims=True)
    row = lax.broadcasted_iota(jnp.int32, (8, TOK), 0)
    small = jnp.where(row == 4, squares, logits)
    high = small.astype(BF16).astype(F32)
    stats = jnp.concatenate([low16, dlow16, high, small - high], axis=0).astype(BF16)
    for k in range(GROUPS):
        out_ref[k, 2 * CAP :, :] = stats
    for copy in early:
        copy.wait()


def weights_kernel(gain_ref, *refs):
    sources, gain_out, targets, sem, gain_sem = refs[:3], refs[3], refs[4:7], refs[7], refs[8]
    copies = [pltpu.make_async_copy(gain_ref, gain_out, gain_sem)]
    for i, (source, target) in enumerate(zip(sources, targets)):
        skipped = source.shape[0] - target.shape[0]
        size = target.shape[0] // 4
        for k in range(4):
            there, here = slice(skipped + k * size, skipped + (k + 1) * size), slice(k * size, (k + 1) * size)
            copies.append(pltpu.make_async_copy(source.at[there], target.at[here], sem.at[i, k]))
    for copy in copies:
        copy.start()
    for copy in copies:
        copy.wait()


CHUNKS = tuple((at, min(256, HIDDEN - at)) for at in range(0, HIDDEN, 256))


def expert_kernel(own_ref, other_ref, gain_ref, wg_ref, wu_ref, wd_ref, early_ref, own_out, other_out, x_s, g_s, da_s, db_s):
    for d, ref in enumerate((own_ref, other_ref)):
        rows = slice(d * CAP, (d + 1) * CAP)
        total = jnp.zeros((CAP, 128), F32)
        for c in range(GROUPS):
            v = ref[c, 0:CAP, :].astype(F32)
            total = total + v * v
        scale = lax.rsqrt(jnp.sum(total, axis=1, keepdims=True) / MODEL_WIDTH + EPS)
        for c in range(GROUPS):
            cols = slice(c * 128, (c + 1) * 128)
            x_s[rows, cols] = (ref[stand(c), 0:CAP, :].astype(F32) * scale * gain_ref[:, cols]).astype(BF16)
            g_s[rows, cols] = ref[stand(c), CAP : 2 * CAP, :]
    gate_terms = jnp.zeros((2 * CAP, 128), F32)
    stat_terms = jnp.zeros((2 * CAP, 128), F32)
    for lower, size in CHUNKS:
        cols = slice(lower, lower + size)
        a = dot(x_s[...], wg_ref[:, cols], 1, 0)
        b = dot(x_s[...], wu_ref[:, cols], 1, 0)
        wd = early_ref[cols, :] if lower < EARLY else wd_ref[lower - EARLY : lower - EARLY + size, :]
        back = dot(g_s[...], wd, 1, 1)
        sig = jax.nn.sigmoid(a)
        act = a * sig
        da = back * b * sig * (1.0 + a * (1.0 - sig))
        db = back * act
        gate = act * b * back
        stat = da * a + db * b
        for k in range(0, size, 128):
            gate_terms = gate_terms + gate[:, k : k + 128]
            stat_terms = stat_terms + stat[:, k : k + 128]
        da_s[:, cols] = da.astype(BF16)
        db_s[:, cols] = db.astype(BF16)
    lane = lax.broadcasted_iota(jnp.int32, (2 * CAP, 128), 1)
    dgate = jnp.sum(gate_terms, axis=1, keepdims=True)
    dstat = jnp.sum(stat_terms, axis=1, keepdims=True)
    table = jnp.where(lane == 0, dgate, jnp.where(lane == 1, dstat, 0.0))
    row = lax.broadcasted_iota(jnp.int32, (8, 128), 0)
    for d, out in enumerate((own_out, other_out)):
        part = jnp.concatenate([table[d * CAP : (d + 1) * CAP], jnp.zeros((128 - CAP, 128), F32)], axis=0)
        lines = part.T[0:8]
        high = lines.astype(BF16).astype(F32)
        packed = jnp.where(row < 2, high, 0.0) + jnp.where((row >= 2) & (row < 4), jnp.roll(lines - high, 2, 0), 0.0)
        packed = jnp.concatenate([packed, jnp.zeros((8, 128), F32)] if d == 0 else [jnp.zeros((8, 128), F32), packed], axis=0)
        for c in range(GROUPS):
            out[c, CAP:BACK, :] = packed.astype(out.dtype)
    for lower in range(0, MODEL_WIDTH, 256):
        rows = slice(lower, lower + 256)
        dn = dot(da_s[...], wg_ref[rows, :], 1, 1) + dot(db_s[...], wu_ref[rows, :], 1, 1)
        for k in range(2):
            c = lower // 128 + k
            own_out[stand(c), 0:CAP, :] = dn[0:CAP, k * 128 : (k + 1) * 128]
            other_out[stand(c), 0:CAP, :] = dn[CAP:, k * 128 : (k + 1) * 128].astype(BF16)


def stats_kernel(
    column, block, lengths, own_ref, other_ref, x_ref, g_ref, xo_ref, go_ref, routes_ref, gain_ref, down_ref, router_ref,
    grad_down_ref, grad_up_ref, side_ref, base_ref, sb_ref, take_ref, hits_ref, routed_ref,
):
    grad_down = jnp.zeros((JOBS * RANK, COLS), F32)
    grad_up = jnp.zeros((JOBS * RANK, COLS), F32)
    gain = local_columns(gain_ref, column[0])
    row = lax.broadcasted_iota(jnp.int32, (8, TOK), 0)
    for d, (ref, xr, gr) in enumerate(((own_ref, x_ref, g_ref), (other_ref, xo_ref, go_ref))):
        total = ref[0, 2 * CAP :, :].astype(F32)
        for c in range(1, GROUPS):
            total = total + ref[c, 2 * CAP :, :].astype(F32)
        small = total[32:40] + total[40:48]
        scale = lax.rsqrt(small[4:5] / MODEL_WIDTH + EPS)
        mask = owner_mask(lengths, (block[0] if d == 0 else 1 - block[0]) * TOK, TOK)
        low16 = total[0:16]
        dlow16 = ADAPTER_SCALE * total[16:32]
        low = jnp.where(mask, jnp.concatenate([low16 * scale] * JOBS, axis=0), 0.0).astype(BF16)
        dlow = jnp.where(mask, jnp.concatenate([dlow16] * JOBS, axis=0), 0.0).astype(BF16)
        if d == 0:
            routes = routes_ref[...]
            label, member, rank = members(routes)
            first = label == routes[0:1]
            second = label == routes[1:2]
            raw = jnp.sum(jnp.where(first, small, 0.0) - jnp.where(second, small, 0.0), axis=0, keepdims=True)
            upper = jax.nn.sigmoid(raw * scale)
            adapter_stat = jnp.sum(dlow16.astype(BF16).astype(F32) * low16, axis=0, keepdims=True)
            at1 = jnp.sum(jnp.where(first, rank, 0.0), axis=0, keepdims=True)
            at2 = jnp.sum(jnp.where(second, rank, 0.0), axis=0, keepdims=True)
            lines = [scale, adapter_stat, raw, upper, at1, at2, routes[0:1].astype(F32), routes[1:2].astype(F32)]
        else:
            lines = [scale] * 8
        packed = jnp.zeros((8, TOK), F32)
        for k, line in enumerate(lines):
            packed = jnp.where(row == k, line, packed)
        side = jnp.concatenate([packed, jnp.zeros((120, TOK), F32)], axis=0).T
        scale_col = side[:, 0:1]
        xf = xr[...].astype(F32)
        normed = (xf * scale_col * gain).astype(BF16)
        grad_down = grad_down + dot(dlow, normed, 1, 0)
        grad_up = grad_up + dot(low, gr[...], 1, 0)
        if d == 0:
            side_ref[...] = side
            wide = jnp.concatenate([down_ref[...].astype(F32), jnp.zeros((64, COLS), F32)], axis=0)
            adapter = dot(wide.T.astype(BF16)[:, 0 : JOBS * RANK], dlow, 1, 0).T
            base_ref[...] = gr[...].astype(F32) + scale_col * adapter * gain
            sb_ref[...] = xf * scale_col * scale_col * scale_col / MODEL_WIDTH
            lane = lax.broadcasted_iota(jnp.int32, (TOK, 128), 1)
            upper = side[:, 3:4]
            at1, at2 = side[:, 4:5].astype(jnp.int32), side[:, 5:6].astype(jnp.int32)
            first, second = side[:, 6:7].astype(jnp.int32), side[:, 7:8].astype(jnp.int32)
            router = local_columns(router_ref, column[0]).astype(F32)
            routed = jnp.zeros((TOK, COLS), F32)
            for e in range(EXPERTS):
                hit1 = ((lane == at1) & (first == e)).astype(F32)
                hit2 = ((lane == at2) & (second == e)).astype(F32)
                take = upper * hit1 + (1.0 - upper) * hit2
                high = take.astype(BF16)
                take_ref[0, e] = high
                take_ref[1, e] = (take - high.astype(F32)).astype(BF16)
                hits_ref[0, e] = take
                hits_ref[1, e] = hit1 - hit2
                sign = (first == e).astype(F32) - (second == e).astype(F32)
                routed = routed + sign * router[e : e + 1]
            routed_ref[...] = routed
    grad_down_ref[...] = grad_down
    grad_up_ref[...] = ADAPTER_SCALE * grad_up


def finish_kernel(column, in_ref, gain_ref, side_ref, base_ref, sb_ref, take_ref, hits_ref, routed_ref, out_ref):
    side = side_ref[...]
    scale, adapter_stat, raw, upper = (side[:, k : k + 1] for k in range(4))
    rows = jnp.zeros((TOK, COLS), F32)
    spread = jnp.zeros((TOK, 128), F32)
    stat = jnp.zeros((TOK, 128), F32)
    for e in range(EXPERTS):
        total = in_ref[stand(4 * e)].astype(F32)
        for k in range(1, 4):
            total = total + in_ref[stand(4 * e + k)].astype(F32)
        lines = total[CAP : CAP + 8] + total[CAP + 8 : CAP + 16]
        spread = spread + hits_ref[1, e] * (lines[0:1] + lines[2:3])
        stat = stat + hits_ref[0, e] * (lines[1:2] + lines[3:4])
        high, low = high_low(total[0:CAP])
        take = take_ref[0, e, :, 0:CAP]
        rows = rows + dot(take, high, 1, 0) + dot(take, low, 1, 0) + dot(take_ref[1, e, :, 0:CAP], high, 1, 0)
    delta = jnp.sum(spread, axis=1, keepdims=True) * upper * (1.0 - upper)
    stat = jnp.sum(stat, axis=1, keepdims=True) / scale + adapter_stat + delta * raw
    dnormed = rows + delta * routed_ref[...]
    result = base_ref[...] + scale * dnormed * local_columns(gain_ref, column[0]) - sb_ref[...] * stat
    out_ref[...] = result.astype(BF16)


VMEM = pl.BlockSpec(memory_space=pltpu.VMEM)
SMEM = pl.BlockSpec(memory_space=pltpu.SMEM)
HBM = pl.BlockSpec(memory_space=pltpu.HBM)


def pinned(v):
    return pltpu.with_memory_space_constraint(v, pltpu.HBM)


def call(kernel, out_shape, scalars, args, scratch=(), arg_specs=None):
    return pl.pallas_call(
        kernel,
        in_specs=[SMEM] * len(scalars) + (arg_specs or [VMEM] * len(args)),
        out_specs=VMEM if isinstance(out_shape, jax.ShapeDtypeStruct) else (VMEM,) * len(out_shape),
        out_shape=out_shape,
        scratch_shapes=scratch,
        compiler_params=pltpu.CompilerParams(vmem_limit_bytes=32 * 1024 * 1024),
    )(*scalars, *(pinned(v) if spec is HBM else v for v, spec in zip(args, arg_specs or [VMEM] * len(args))))


def shards(stash, cotangent, routes, lengths, gains, router, wg, wu, wd, down, up):
    x, g = stash[0], cotangent[0]
    routes, router, down = routes[0].T, router[0].T, down[0].T
    wg, wu, wd, up = wg[0], wu[0], wd[0], up[0]
    shape = jax.ShapeDtypeStruct
    column = lax.axis_index(EXPERT).astype(jnp.int32).reshape(1)
    block = lax.axis_index("dp").astype(jnp.int32).reshape(1)
    swap = [(0, 1), (1, 0)]
    xo = lax.ppermute(x, "dp", swap)
    go = lax.ppermute(g, "dp", swap)
    locals_ = (lengths, x, g, routes, gains, router, down, up)
    sent, early = call(
        prepare_kernel,
        (shape((GROUPS, SEND, 128), BF16), shape((EARLY, MODEL_WIDTH), BF16)),
        (column, block),
        (*locals_, wd),
        [pltpu.SMEM(lengths.shape, jnp.int32)]
        + [pltpu.VMEM(v.shape, v.dtype) for v in locals_[1:]]
        + [pltpu.SemaphoreType.DMA((8 + EARLY // 128,))],
        [HBM] * 9,
    )
    own = lax.all_to_all(sent, EXCHANGE, 0, 0, tiled=True)
    other = lax.ppermute(own, "dp", swap)
    gains_here, *weights = call(
        weights_kernel,
        (
            shape(gains.shape, F32), shape(wg.shape, BF16), shape(wu.shape, BF16),
            shape((HIDDEN - EARLY, MODEL_WIDTH), BF16),
        ),
        (),
        (gains, wg, wu, wd),
        [pltpu.SemaphoreType.DMA((3, 4)), pltpu.SemaphoreType.DMA],
        [HBM] * 4,
    )
    other, xo, go = lax.optimization_barrier((other, xo, go))
    own_part, other_part = call(
        expert_kernel,
        (shape((GROUPS, BACK, 128), F32), shape((GROUPS, BACK, 128), BF16)),
        (),
        (own, other, gains_here, *weights, early),
        [
            pltpu.VMEM((2 * CAP, MODEL_WIDTH), BF16),
            pltpu.VMEM((2 * CAP, MODEL_WIDTH), BF16),
            pltpu.VMEM((2 * CAP, HIDDEN), BF16),
            pltpu.VMEM((2 * CAP, HIDDEN), BF16),
        ],
    )
    arrived = lax.ppermute(other_part, "dp", swap)
    small = shape((JOBS * RANK, COLS), F32)
    square = shape((TOK, COLS), F32)
    grad_down, grad_up, side, base, sb, take, hits, routed = call(
        stats_kernel,
        (
            small, small, square, square, square,
            shape((2, EXPERTS, TOK, 128), BF16), shape((2, EXPERTS, TOK, 128), F32), square,
        ),
        (column, block, lengths),
        (own, other, x, g, xo, go, routes, gains, down, router),
    )
    arrived, side = lax.optimization_barrier((arrived, side))
    parts = (own_part + arrived.astype(F32)).astype(BF16)
    back = lax.all_to_all(parts, EXCHANGE, 0, 0, tiled=True)
    result = call(
        finish_kernel,
        shape((TOK, COLS), BF16),
        (column,),
        (back, gains, side, base, sb, take, hits, routed),
    )
    count = lax.axis_size("section")
    handed = lax.ppermute(result, "section", [(i, (i - 1) % count) for i in range(count)])
    return handed[None], grad_down.T[None], grad_up[None]


def solution(mesh):
    finer = Mesh(
        mesh.devices.reshape(mesh.shape["section"], 4, 4, mesh.shape["dp"]),
        ("section", "expert_0", "expert_1", "dp"),
    )
    in_specs = (
        P("section", "dp", EXPERT),
        P("section", "dp", EXPERT),
        P("section", "dp", None),
        P("section", None),
        P("section", None),
        P("section", None, None),
        P("section", None, EXPERT_DP),
        P("section", None, EXPERT_DP),
        P("section", EXPERT_DP, None),
        P("section", EXPERT, None),
        P("section", None, EXPERT),
    )
    out_specs = (P("section", "dp", EXPERT), P("section", EXPERT, None), P("section", None, EXPERT))
    return jax.shard_map(shards, mesh=finer, in_specs=in_specs, out_specs=out_specs, check_vma=False)
```

```python
import jax
import jax.numpy as jnp
from jax import lax
from jax.experimental import pallas as pl
from jax.experimental.pallas import tpu as pltpu
from jax.sharding import Mesh
from jax.sharding import PartitionSpec as P

MODEL_WIDTH = 2048
EXPERTS = 4
RANK = 16
JOBS = 4
CAP = 80
TOK = 128
COLS = 128
GROUPS = 16
STATS = 48
SEND = 2 * CAP + STATS
BACK = CAP + 16
HIDDEN = 896
EARLY = 256
EXPERT = ("expert_0", "expert_1")
EXCHANGE = ("expert_1", "expert_0")
EXPERT_DP = ("expert_0", "expert_1", "dp")
EPS = 1e-05
ADAPTER_SCALE = 0.5
F32 = jnp.float32
BF16 = jnp.bfloat16


def dot(a, b, ca, cb):
    return lax.dot_general(a, b, (((ca,), (cb,)), ((), ())), preferred_element_type=F32)


def stand(c):
    return c % 4 * 4 + c // 4


def high_low(v):
    high = v.astype(BF16)
    return high, (v - high.astype(F32)).astype(BF16)


def members(routes):
    label = lax.broadcasted_iota(jnp.int32, (8, TOK), 0)
    member = (label == routes[0:1]) | (label == routes[1:2])
    earlier = (
        lax.broadcasted_iota(jnp.int32, (TOK, TOK), 0)
        < lax.broadcasted_iota(jnp.int32, (TOK, TOK), 1)
    ).astype(BF16)
    rank = dot(member.astype(BF16), earlier, 1, 0)
    return label, member, rank


def owner_mask(lengths, offset, count):
    token = offset + lax.broadcasted_iota(jnp.int32, (JOBS * RANK, count), 1)
    job = lax.broadcasted_iota(jnp.int32, (JOBS * RANK, count), 0) // RANK
    owner = jnp.zeros((JOBS * RANK, count), jnp.int32)
    end = jnp.int32(0)
    for j in range(JOBS):
        end = end + lengths[0, j]
        owner = owner + (token >= end).astype(jnp.int32)
    return owner == job


def local_columns(ref, column):
    return ref[:, pl.ds(pl.multiple_of(column * COLS, COLS), COLS)]


def prepare_kernel(column, block, *refs):
    sources, wd_hbm, out_ref, early_ref, pair_ref, sem = refs[:8], refs[8], refs[9], refs[10], refs[11], refs[20]
    lengths, x_ref, g_ref, routes_ref, gain_ref, router_ref, down_ref, up_ref = refs[12:20]
    copies = [pltpu.make_async_copy(a, b, sem.at[i]) for i, (a, b) in enumerate(zip(sources, refs[12:20]))]
    early = []
    for k in range(EARLY // 128):
        rows = slice(k * 128, (k + 1) * 128)
        early.append(pltpu.make_async_copy(wd_hbm.at[rows], early_ref.at[rows], sem.at[8 + k]))
    for copy in copies:
        copy.start()
    for copy in early:
        copy.start()
    for copy in copies:
        copy.wait()
    x = x_ref[...]
    g = g_ref[...]
    pair_ref[0] = x
    pair_ref[1] = g
    _, member, rank = members(routes_ref[...])
    slot = lax.broadcasted_iota(jnp.int32, (CAP, TOK), 0)
    place = jnp.where(member, rank.astype(jnp.int32), -1)
    for e in range(EXPERTS):
        pick = (place[e : e + 1] == slot).astype(BF16)
        xs = dot(pick, x, 1, 0).astype(BF16)
        gs = dot(pick, g, 1, 0).astype(BF16)
        for k in range(GROUPS // EXPERTS):
            out_ref[stand(e * 4 + k), 0:CAP, :] = xs
            out_ref[stand(e * 4 + k), CAP : 2 * CAP, :] = gs
    xf = x.astype(F32)
    xg = (xf * local_columns(gain_ref, column[0])).astype(BF16)
    mask = owner_mask(lengths, block[0] * TOK, TOK)
    low = jnp.where(mask, dot(down_ref[...], xg, 1, 1), 0.0)
    dlow = jnp.where(mask, dot(up_ref[...], g, 1, 1), 0.0)
    low16 = low[0:16] + low[16:32] + low[32:48] + low[48:64]
    dlow16 = dlow[0:16] + dlow[16:32] + dlow[32:48] + dlow[48:64]
    router = local_columns(router_ref, column[0]).astype(F32)
    wide = jnp.concatenate([router, jnp.zeros((4, COLS), F32)], axis=0)
    logits = dot(wide.astype(BF16), xg, 1, 1)
    square = xf * xf
    squares = jnp.sum(square.T, axis=0, keepdims=True)
    row = lax.broadcasted_iota(jnp.int32, (8, TOK), 0)
    small = jnp.where(row == 4, squares, logits)
    high = small.astype(BF16).astype(F32)
    stats = jnp.concatenate([low16, dlow16, high, small - high], axis=0).astype(BF16)
    for k in range(GROUPS):
        out_ref[k, 2 * CAP :, :] = stats
    for copy in early:
        copy.wait()


def weights_kernel(gain_ref, *refs):
    sources, gain_out, targets, sem, gain_sem = refs[:3], refs[3], refs[4:7], refs[7], refs[8]
    copies = [pltpu.make_async_copy(gain_ref, gain_out, gain_sem)]
    for i, (source, target) in enumerate(zip(sources, targets)):
        skipped = source.shape[0] - target.shape[0]
        size = target.shape[0] // 4
        for k in range(4):
            there, here = slice(skipped + k * size, skipped + (k + 1) * size), slice(k * size, (k + 1) * size)
            copies.append(pltpu.make_async_copy(source.at[there], target.at[here], sem.at[i, k]))
    for copy in copies:
        copy.start()
    for copy in copies:
        copy.wait()


CHUNKS = tuple((at, min(256, HIDDEN - at)) for at in range(0, HIDDEN, 256))


def expert_kernel(own_ref, other_ref, gain_ref, wg_ref, wu_ref, wd_ref, early_ref, own_out, other_out, x_s, g_s, da_s, db_s):
    for d, ref in enumerate((own_ref, other_ref)):
        rows = slice(d * CAP, (d + 1) * CAP)
        total = jnp.zeros((CAP, 128), F32)
        for c in range(GROUPS):
            v = ref[c, 0:CAP, :].astype(F32)
            total = total + v * v
        scale = lax.rsqrt(jnp.sum(total, axis=1, keepdims=True) / MODEL_WIDTH + EPS)
        for c in range(GROUPS):
            cols = slice(c * 128, (c + 1) * 128)
            x_s[rows, cols] = (ref[stand(c), 0:CAP, :].astype(F32) * scale * gain_ref[:, cols]).astype(BF16)
            g_s[rows, cols] = ref[stand(c), CAP : 2 * CAP, :]
    gate_terms = jnp.zeros((2 * CAP, 128), F32)
    stat_terms = jnp.zeros((2 * CAP, 128), F32)
    for lower, size in CHUNKS:
        cols = slice(lower, lower + size)
        a = dot(x_s[...], wg_ref[:, cols], 1, 0)
        b = dot(x_s[...], wu_ref[:, cols], 1, 0)
        wd = early_ref[cols, :] if lower < EARLY else wd_ref[lower - EARLY : lower - EARLY + size, :]
        back = dot(g_s[...], wd, 1, 1)
        sig = jax.nn.sigmoid(a)
        act = a * sig
        da = back * b * sig * (1.0 + a * (1.0 - sig))
        db = back * act
        gate = act * b * back
        stat = da * a + db * b
        for k in range(0, size, 128):
            gate_terms = gate_terms + gate[:, k : k + 128]
            stat_terms = stat_terms + stat[:, k : k + 128]
        da_s[:, cols] = da.astype(BF16)
        db_s[:, cols] = db.astype(BF16)
    lane = lax.broadcasted_iota(jnp.int32, (2 * CAP, 128), 1)
    dgate = jnp.sum(gate_terms, axis=1, keepdims=True)
    dstat = jnp.sum(stat_terms, axis=1, keepdims=True)
    table = jnp.where(lane == 0, dgate, jnp.where(lane == 1, dstat, 0.0))
    row = lax.broadcasted_iota(jnp.int32, (8, 128), 0)
    for d, out in enumerate((own_out, other_out)):
        part = jnp.concatenate([table[d * CAP : (d + 1) * CAP], jnp.zeros((128 - CAP, 128), F32)], axis=0)
        lines = part.T[0:8]
        high = lines.astype(BF16).astype(F32)
        packed = jnp.where(row < 2, high, 0.0) + jnp.where((row >= 2) & (row < 4), jnp.roll(lines - high, 2, 0), 0.0)
        packed = jnp.concatenate([packed, jnp.zeros((8, 128), F32)] if d == 0 else [jnp.zeros((8, 128), F32), packed], axis=0)
        for c in range(GROUPS):
            out[c, CAP:BACK, :] = packed.astype(out.dtype)
    for lower in range(0, MODEL_WIDTH, 256):
        rows = slice(lower, lower + 256)
        dn = dot(da_s[...], wg_ref[rows, :], 1, 1) + dot(db_s[...], wu_ref[rows, :], 1, 1)
        for k in range(2):
            c = lower // 128 + k
            own_out[stand(c), 0:CAP, :] = dn[0:CAP, k * 128 : (k + 1) * 128]
            other_out[stand(c), 0:CAP, :] = dn[CAP:, k * 128 : (k + 1) * 128].astype(BF16)


def stats_kernel(
    column, block, lengths, own_ref, other_ref, x_ref, g_ref, pair_ref, routes_ref, gain_ref, down_ref, router_ref,
    grad_down_ref, grad_up_ref, side_ref, base_ref, sb_ref, take_ref, hits_ref, routed_ref,
):
    grad_down = jnp.zeros((JOBS * RANK, COLS), F32)
    grad_up = jnp.zeros((JOBS * RANK, COLS), F32)
    gain = local_columns(gain_ref, column[0])
    row = lax.broadcasted_iota(jnp.int32, (8, TOK), 0)
    for d, (ref, xr, gr) in enumerate(((own_ref, x_ref, g_ref), (other_ref, pair_ref.at[0], pair_ref.at[1]))):
        total = ref[0, 2 * CAP :, :].astype(F32)
        for c in range(1, GROUPS):
            total = total + ref[c, 2 * CAP :, :].astype(F32)
        small = total[32:40] + total[40:48]
        scale = lax.rsqrt(small[4:5] / MODEL_WIDTH + EPS)
        mask = owner_mask(lengths, (block[0] if d == 0 else 1 - block[0]) * TOK, TOK)
        low16 = total[0:16]
        dlow16 = ADAPTER_SCALE * total[16:32]
        low = jnp.where(mask, jnp.concatenate([low16 * scale] * JOBS, axis=0), 0.0).astype(BF16)
        dlow = jnp.where(mask, jnp.concatenate([dlow16] * JOBS, axis=0), 0.0).astype(BF16)
        if d == 0:
            routes = routes_ref[...]
            label, member, rank = members(routes)
            first = label == routes[0:1]
            second = label == routes[1:2]
            raw = jnp.sum(jnp.where(first, small, 0.0) - jnp.where(second, small, 0.0), axis=0, keepdims=True)
            upper = jax.nn.sigmoid(raw * scale)
            adapter_stat = jnp.sum(dlow16.astype(BF16).astype(F32) * low16, axis=0, keepdims=True)
            at1 = jnp.sum(jnp.where(first, rank, 0.0), axis=0, keepdims=True)
            at2 = jnp.sum(jnp.where(second, rank, 0.0), axis=0, keepdims=True)
            lines = [scale, adapter_stat, raw, upper, at1, at2, routes[0:1].astype(F32), routes[1:2].astype(F32)]
        else:
            lines = [scale] * 8
        packed = jnp.zeros((8, TOK), F32)
        for k, line in enumerate(lines):
            packed = jnp.where(row == k, line, packed)
        side = jnp.concatenate([packed, jnp.zeros((120, TOK), F32)], axis=0).T
        scale_col = side[:, 0:1]
        xf = xr[...].astype(F32)
        normed = (xf * scale_col * gain).astype(BF16)
        grad_down = grad_down + dot(dlow, normed, 1, 0)
        grad_up = grad_up + dot(low, gr[...], 1, 0)
        if d == 0:
            side_ref[...] = side
            wide = jnp.concatenate([down_ref[...].astype(F32), jnp.zeros((64, COLS), F32)], axis=0)
            adapter = dot(wide.T.astype(BF16)[:, 0 : JOBS * RANK], dlow, 1, 0).T
            base_ref[...] = gr[...].astype(F32) + scale_col * adapter * gain
            sb_ref[...] = xf * scale_col * scale_col * scale_col / MODEL_WIDTH
            lane = lax.broadcasted_iota(jnp.int32, (TOK, 128), 1)
            upper = side[:, 3:4]
            at1, at2 = side[:, 4:5].astype(jnp.int32), side[:, 5:6].astype(jnp.int32)
            first, second = side[:, 6:7].astype(jnp.int32), side[:, 7:8].astype(jnp.int32)
            router = local_columns(router_ref, column[0]).astype(F32)
            routed = jnp.zeros((TOK, COLS), F32)
            for e in range(EXPERTS):
                hit1 = ((lane == at1) & (first == e)).astype(F32)
                hit2 = ((lane == at2) & (second == e)).astype(F32)
                take = upper * hit1 + (1.0 - upper) * hit2
                high = take.astype(BF16)
                take_ref[0, e] = high
                take_ref[1, e] = (take - high.astype(F32)).astype(BF16)
                hits_ref[0, e] = take
                hits_ref[1, e] = hit1 - hit2
                sign = (first == e).astype(F32) - (second == e).astype(F32)
                routed = routed + sign * router[e : e + 1]
            routed_ref[...] = routed
    grad_down_ref[...] = grad_down
    grad_up_ref[...] = ADAPTER_SCALE * grad_up


def finish_kernel(column, in_ref, gain_ref, side_ref, base_ref, sb_ref, take_ref, hits_ref, routed_ref, out_ref):
    side = side_ref[...]
    scale, adapter_stat, raw, upper = (side[:, k : k + 1] for k in range(4))
    rows = jnp.zeros((TOK, COLS), F32)
    spread = jnp.zeros((TOK, 128), F32)
    stat = jnp.zeros((TOK, 128), F32)
    for e in range(EXPERTS):
        total = in_ref[stand(4 * e)].astype(F32)
        for k in range(1, 4):
            total = total + in_ref[stand(4 * e + k)].astype(F32)
        lines = total[CAP : CAP + 8] + total[CAP + 8 : CAP + 16]
        spread = spread + hits_ref[1, e] * (lines[0:1] + lines[2:3])
        stat = stat + hits_ref[0, e] * (lines[1:2] + lines[3:4])
        high, low = high_low(total[0:CAP])
        take = take_ref[0, e, :, 0:CAP]
        rows = rows + dot(take, high, 1, 0) + dot(take, low, 1, 0) + dot(take_ref[1, e, :, 0:CAP], high, 1, 0)
    delta = jnp.sum(spread, axis=1, keepdims=True) * upper * (1.0 - upper)
    stat = jnp.sum(stat, axis=1, keepdims=True) / scale + adapter_stat + delta * raw
    dnormed = rows + delta * routed_ref[...]
    result = base_ref[...] + scale * dnormed * local_columns(gain_ref, column[0]) - sb_ref[...] * stat
    out_ref[...] = result.astype(BF16)


VMEM = pl.BlockSpec(memory_space=pltpu.VMEM)
SMEM = pl.BlockSpec(memory_space=pltpu.SMEM)
HBM = pl.BlockSpec(memory_space=pltpu.HBM)


def pinned(v):
    return pltpu.with_memory_space_constraint(v, pltpu.HBM)


def call(kernel, out_shape, scalars, args, scratch=(), arg_specs=None):
    return pl.pallas_call(
        kernel,
        in_specs=[SMEM] * len(scalars) + (arg_specs or [VMEM] * len(args)),
        out_specs=VMEM if isinstance(out_shape, jax.ShapeDtypeStruct) else (VMEM,) * len(out_shape),
        out_shape=out_shape,
        scratch_shapes=scratch,
        compiler_params=pltpu.CompilerParams(vmem_limit_bytes=32 * 1024 * 1024),
    )(*scalars, *(pinned(v) if spec is HBM else v for v, spec in zip(args, arg_specs or [VMEM] * len(args))))


def shards(stash, cotangent, routes, lengths, gains, router, wg, wu, wd, down, up):
    x, g = stash[0], cotangent[0]
    routes, router, down = routes[0].T, router[0].T, down[0].T
    wg, wu, wd, up = wg[0], wu[0], wd[0], up[0]
    shape = jax.ShapeDtypeStruct
    column = lax.axis_index(EXPERT).astype(jnp.int32).reshape(1)
    block = lax.axis_index("dp").astype(jnp.int32).reshape(1)
    swap = [(0, 1), (1, 0)]
    locals_ = (lengths, x, g, routes, gains, router, down, up)
    sent, early, pair = call(
        prepare_kernel,
        (shape((GROUPS, SEND, 128), BF16), shape((EARLY, MODEL_WIDTH), BF16), shape((2, TOK, COLS), BF16)),
        (column, block),
        (*locals_, wd),
        [pltpu.SMEM(lengths.shape, jnp.int32)]
        + [pltpu.VMEM(v.shape, v.dtype) for v in locals_[1:]]
        + [pltpu.SemaphoreType.DMA((8 + EARLY // 128,))],
        [HBM] * 9,
    )
    own = lax.all_to_all(sent, EXCHANGE, 0, 0, tiled=True)
    other = lax.ppermute(own, "dp", swap)
    gains_here, *weights = call(
        weights_kernel,
        (
            shape(gains.shape, F32), shape(wg.shape, BF16), shape(wu.shape, BF16),
            shape((HIDDEN - EARLY, MODEL_WIDTH), BF16),
        ),
        (),
        (gains, wg, wu, wd),
        [pltpu.SemaphoreType.DMA((3, 4)), pltpu.SemaphoreType.DMA],
        [HBM] * 4,
    )
    other, pair = lax.optimization_barrier((other, lax.ppermute(pair, "dp", swap)))
    own_part, other_part = call(
        expert_kernel,
        (shape((GROUPS, BACK, 128), F32), shape((GROUPS, BACK, 128), BF16)),
        (),
        (own, other, gains_here, *weights, early),
        [
            pltpu.VMEM((2 * CAP, MODEL_WIDTH), BF16),
            pltpu.VMEM((2 * CAP, MODEL_WIDTH), BF16),
            pltpu.VMEM((2 * CAP, HIDDEN), BF16),
            pltpu.VMEM((2 * CAP, HIDDEN), BF16),
        ],
    )
    arrived = lax.ppermute(other_part, "dp", swap)
    small = shape((JOBS * RANK, COLS), F32)
    square = shape((TOK, COLS), F32)
    grad_down, grad_up, side, base, sb, take, hits, routed = call(
        stats_kernel,
        (
            small, small, square, square, square,
            shape((2, EXPERTS, TOK, 128), BF16), shape((2, EXPERTS, TOK, 128), F32), square,
        ),
        (column, block, lengths),
        (own, other, x, g, pair, routes, gains, down, router),
    )
    arrived, side = lax.optimization_barrier((arrived, side))
    parts = (own_part + arrived.astype(F32)).astype(BF16)
    back = lax.all_to_all(parts, EXCHANGE, 0, 0, tiled=True)
    result = call(
        finish_kernel,
        shape((TOK, COLS), BF16),
        (column,),
        (back, gains, side, base, sb, take, hits, routed),
    )
    count = lax.axis_size("section")
    handed = lax.ppermute(result, "section", [(i, (i - 1) % count) for i in range(count)])
    return handed[None], grad_down.T[None], grad_up[None]


def solution(mesh):
    finer = Mesh(
        mesh.devices.reshape(mesh.shape["section"], 4, 4, mesh.shape["dp"]),
        ("section", "expert_0", "expert_1", "dp"),
    )
    in_specs = (
        P("section", "dp", EXPERT),
        P("section", "dp", EXPERT),
        P("section", "dp", None),
        P("section", None),
        P("section", None),
        P("section", None, None),
        P("section", None, EXPERT_DP),
        P("section", None, EXPERT_DP),
        P("section", EXPERT_DP, None),
        P("section", EXPERT, None),
        P("section", None, EXPERT),
    )
    out_specs = (P("section", "dp", EXPERT), P("section", EXPERT, None), P("section", None, EXPERT))
    return jax.shard_map(shards, mesh=finer, in_specs=in_specs, out_specs=out_specs, check_vma=False)
```

```python
import jax
import jax.numpy as jnp
from jax import lax
from jax.experimental import pallas as pl
from jax.experimental.pallas import tpu as pltpu
from jax.sharding import Mesh
from jax.sharding import PartitionSpec as P

MODEL_WIDTH = 2048
EXPERTS = 4
RANK = 16
JOBS = 4
CAP = 80
TOK = 128
COLS = 128
GROUPS = 16
STATS = 48
SEND = 2 * CAP + STATS
BACK = CAP + 16
HIDDEN = 896
EARLY = 512
EXPERT = ("expert_0", "expert_1")
EXCHANGE = ("expert_1", "expert_0")
EXPERT_DP = ("expert_0", "expert_1", "dp")
EPS = 1e-05
ADAPTER_SCALE = 0.5
F32 = jnp.float32
BF16 = jnp.bfloat16


def dot(a, b, ca, cb):
    return lax.dot_general(a, b, (((ca,), (cb,)), ((), ())), preferred_element_type=F32)


def stand(c):
    return c % 4 * 4 + c // 4


def high_low(v):
    high = v.astype(BF16)
    return high, (v - high.astype(F32)).astype(BF16)


def members(routes):
    label = lax.broadcasted_iota(jnp.int32, (8, TOK), 0)
    member = (label == routes[0:1]) | (label == routes[1:2])
    earlier = (
        lax.broadcasted_iota(jnp.int32, (TOK, TOK), 0)
        < lax.broadcasted_iota(jnp.int32, (TOK, TOK), 1)
    ).astype(BF16)
    rank = dot(member.astype(BF16), earlier, 1, 0)
    return label, member, rank


def owner_mask(lengths, offset, count):
    token = offset + lax.broadcasted_iota(jnp.int32, (JOBS * RANK, count), 1)
    job = lax.broadcasted_iota(jnp.int32, (JOBS * RANK, count), 0) // RANK
    owner = jnp.zeros((JOBS * RANK, count), jnp.int32)
    end = jnp.int32(0)
    for j in range(JOBS):
        end = end + lengths[0, j]
        owner = owner + (token >= end).astype(jnp.int32)
    return owner == job


def local_columns(ref, column):
    return ref[:, pl.ds(pl.multiple_of(column * COLS, COLS), COLS)]


def prepare_kernel(column, block, *refs):
    sources, wd_hbm, out_ref, early_ref, pair_ref, sem = refs[:8], refs[8], refs[9], refs[10], refs[11], refs[20]
    lengths, x_ref, g_ref, routes_ref, gain_ref, router_ref, down_ref, up_ref = refs[12:20]
    copies = [pltpu.make_async_copy(a, b, sem.at[i]) for i, (a, b) in enumerate(zip(sources, refs[12:20]))]
    early = []
    for k in range(EARLY // 128):
        rows = slice(k * 128, (k + 1) * 128)
        early.append(pltpu.make_async_copy(wd_hbm.at[rows], early_ref.at[rows], sem.at[8 + k]))
    for copy in copies:
        copy.start()
    for copy in early:
        copy.start()
    for copy in copies:
        copy.wait()
    x = x_ref[...]
    g = g_ref[...]
    pair_ref[0] = x
    pair_ref[1] = g
    _, member, rank = members(routes_ref[...])
    slot = lax.broadcasted_iota(jnp.int32, (CAP, TOK), 0)
    place = jnp.where(member, rank.astype(jnp.int32), -1)
    for e in range(EXPERTS):
        pick = (place[e : e + 1] == slot).astype(BF16)
        xs = dot(pick, x, 1, 0).astype(BF16)
        gs = dot(pick, g, 1, 0).astype(BF16)
        for k in range(GROUPS // EXPERTS):
            out_ref[stand(e * 4 + k), 0:CAP, :] = xs
            out_ref[stand(e * 4 + k), CAP : 2 * CAP, :] = gs
    xf = x.astype(F32)
    xg = (xf * local_columns(gain_ref, column[0])).astype(BF16)
    mask = owner_mask(lengths, block[0] * TOK, TOK)
    low = jnp.where(mask, dot(down_ref[...], xg, 1, 1), 0.0)
    dlow = jnp.where(mask, dot(up_ref[...], g, 1, 1), 0.0)
    low16 = low[0:16] + low[16:32] + low[32:48] + low[48:64]
    dlow16 = dlow[0:16] + dlow[16:32] + dlow[32:48] + dlow[48:64]
    router = local_columns(router_ref, column[0]).astype(F32)
    wide = jnp.concatenate([router, jnp.zeros((4, COLS), F32)], axis=0)
    logits = dot(wide.astype(BF16), xg, 1, 1)
    square = xf * xf
    squares = jnp.sum(square.T, axis=0, keepdims=True)
    row = lax.broadcasted_iota(jnp.int32, (8, TOK), 0)
    small = jnp.where(row == 4, squares, logits)
    high = small.astype(BF16).astype(F32)
    stats = jnp.concatenate([low16, dlow16, high, small - high], axis=0).astype(BF16)
    for k in range(GROUPS):
        out_ref[k, 2 * CAP :, :] = stats
    for copy in early:
        copy.wait()


def weights_kernel(gain_ref, *refs):
    sources, gain_out, targets, sem, gain_sem = refs[:3], refs[3], refs[4:7], refs[7], refs[8]
    copies = [pltpu.make_async_copy(gain_ref, gain_out, gain_sem)]
    for i, (source, target) in enumerate(zip(sources, targets)):
        skipped = source.shape[0] - target.shape[0]
        size = target.shape[0] // 4
        for k in range(4):
            there, here = slice(skipped + k * size, skipped + (k + 1) * size), slice(k * size, (k + 1) * size)
            copies.append(pltpu.make_async_copy(source.at[there], target.at[here], sem.at[i, k]))
    for copy in copies:
        copy.start()
    for copy in copies:
        copy.wait()


CHUNKS = tuple((at, min(256, HIDDEN - at)) for at in range(0, HIDDEN, 256))


def expert_kernel(own_ref, other_ref, gain_ref, wg_ref, wu_ref, wd_ref, early_ref, own_out, other_out, x_s, g_s, da_s, db_s):
    for d, ref in enumerate((own_ref, other_ref)):
        rows = slice(d * CAP, (d + 1) * CAP)
        total = jnp.zeros((CAP, 128), F32)
        for c in range(GROUPS):
            v = ref[c, 0:CAP, :].astype(F32)
            total = total + v * v
        scale = lax.rsqrt(jnp.sum(total, axis=1, keepdims=True) / MODEL_WIDTH + EPS)
        for c in range(GROUPS):
            cols = slice(c * 128, (c + 1) * 128)
            x_s[rows, cols] = (ref[stand(c), 0:CAP, :].astype(F32) * scale * gain_ref[:, cols]).astype(BF16)
            g_s[rows, cols] = ref[stand(c), CAP : 2 * CAP, :]
    gate_terms = jnp.zeros((2 * CAP, 128), F32)
    stat_terms = jnp.zeros((2 * CAP, 128), F32)
    for lower, size in CHUNKS:
        cols = slice(lower, lower + size)
        a = dot(x_s[...], wg_ref[:, cols], 1, 0)
        b = dot(x_s[...], wu_ref[:, cols], 1, 0)
        wd = early_ref[cols, :] if lower < EARLY else wd_ref[lower - EARLY : lower - EARLY + size, :]
        back = dot(g_s[...], wd, 1, 1)
        sig = jax.nn.sigmoid(a)
        act = a * sig
        da = back * b * sig * (1.0 + a * (1.0 - sig))
        db = back * act
        gate = act * b * back
        stat = da * a + db * b
        for k in range(0, size, 128):
            gate_terms = gate_terms + gate[:, k : k + 128]
            stat_terms = stat_terms + stat[:, k : k + 128]
        da_s[:, cols] = da.astype(BF16)
        db_s[:, cols] = db.astype(BF16)
    lane = lax.broadcasted_iota(jnp.int32, (2 * CAP, 128), 1)
    dgate = jnp.sum(gate_terms, axis=1, keepdims=True)
    dstat = jnp.sum(stat_terms, axis=1, keepdims=True)
    table = jnp.where(lane == 0, dgate, jnp.where(lane == 1, dstat, 0.0))
    row = lax.broadcasted_iota(jnp.int32, (8, 128), 0)
    for d, out in enumerate((own_out, other_out)):
        part = jnp.concatenate([table[d * CAP : (d + 1) * CAP], jnp.zeros((128 - CAP, 128), F32)], axis=0)
        lines = part.T[0:8]
        high = lines.astype(BF16).astype(F32)
        packed = jnp.where(row < 2, high, 0.0) + jnp.where((row >= 2) & (row < 4), jnp.roll(lines - high, 2, 0), 0.0)
        packed = jnp.concatenate([packed, jnp.zeros((8, 128), F32)] if d == 0 else [jnp.zeros((8, 128), F32), packed], axis=0)
        for c in range(GROUPS):
            out[c, CAP:BACK, :] = packed.astype(out.dtype)
    for lower in range(0, MODEL_WIDTH, 256):
        rows = slice(lower, lower + 256)
        dn = dot(da_s[...], wg_ref[rows, :], 1, 1) + dot(db_s[...], wu_ref[rows, :], 1, 1)
        for k in range(2):
            c = lower // 128 + k
            own_out[stand(c), 0:CAP, :] = dn[0:CAP, k * 128 : (k + 1) * 128]
            other_out[stand(c), 0:CAP, :] = dn[CAP:, k * 128 : (k + 1) * 128].astype(BF16)


def stats_kernel(
    column, block, lengths, own_ref, other_ref, x_ref, g_ref, pair_ref, routes_ref, gain_ref, down_ref, router_ref,
    grad_down_ref, grad_up_ref, side_ref, base_ref, sb_ref, take_ref, hits_ref, routed_ref,
):
    grad_down = jnp.zeros((JOBS * RANK, COLS), F32)
    grad_up = jnp.zeros((JOBS * RANK, COLS), F32)
    gain = local_columns(gain_ref, column[0])
    row = lax.broadcasted_iota(jnp.int32, (8, TOK), 0)
    for d, (ref, xr, gr) in enumerate(((own_ref, x_ref, g_ref), (other_ref, pair_ref.at[0], pair_ref.at[1]))):
        total = ref[0, 2 * CAP :, :].astype(F32)
        for c in range(1, GROUPS):
            total = total + ref[c, 2 * CAP :, :].astype(F32)
        small = total[32:40] + total[40:48]
        scale = lax.rsqrt(small[4:5] / MODEL_WIDTH + EPS)
        mask = owner_mask(lengths, (block[0] if d == 0 else 1 - block[0]) * TOK, TOK)
        low16 = total[0:16]
        dlow16 = ADAPTER_SCALE * total[16:32]
        low = jnp.where(mask, jnp.concatenate([low16 * scale] * JOBS, axis=0), 0.0).astype(BF16)
        dlow = jnp.where(mask, jnp.concatenate([dlow16] * JOBS, axis=0), 0.0).astype(BF16)
        if d == 0:
            routes = routes_ref[...]
            label, member, rank = members(routes)
            first = label == routes[0:1]
            second = label == routes[1:2]
            raw = jnp.sum(jnp.where(first, small, 0.0) - jnp.where(second, small, 0.0), axis=0, keepdims=True)
            upper = jax.nn.sigmoid(raw * scale)
            adapter_stat = jnp.sum(dlow16.astype(BF16).astype(F32) * low16, axis=0, keepdims=True)
            at1 = jnp.sum(jnp.where(first, rank, 0.0), axis=0, keepdims=True)
            at2 = jnp.sum(jnp.where(second, rank, 0.0), axis=0, keepdims=True)
            lines = [scale, adapter_stat, raw, upper, at1, at2, routes[0:1].astype(F32), routes[1:2].astype(F32)]
        else:
            lines = [scale] * 8
        packed = jnp.zeros((8, TOK), F32)
        for k, line in enumerate(lines):
            packed = jnp.where(row == k, line, packed)
        side = jnp.concatenate([packed, jnp.zeros((120, TOK), F32)], axis=0).T
        scale_col = side[:, 0:1]
        xf = xr[...].astype(F32)
        normed = (xf * scale_col * gain).astype(BF16)
        grad_down = grad_down + dot(dlow, normed, 1, 0)
        grad_up = grad_up + dot(low, gr[...], 1, 0)
        if d == 0:
            side_ref[...] = side
            wide = jnp.concatenate([down_ref[...].astype(F32), jnp.zeros((64, COLS), F32)], axis=0)
            adapter = dot(wide.T.astype(BF16)[:, 0 : JOBS * RANK], dlow, 1, 0).T
            base_ref[...] = gr[...].astype(F32) + scale_col * adapter * gain
            sb_ref[...] = xf * scale_col * scale_col * scale_col / MODEL_WIDTH
            lane = lax.broadcasted_iota(jnp.int32, (TOK, 128), 1)
            upper = side[:, 3:4]
            at1, at2 = side[:, 4:5].astype(jnp.int32), side[:, 5:6].astype(jnp.int32)
            first, second = side[:, 6:7].astype(jnp.int32), side[:, 7:8].astype(jnp.int32)
            router = local_columns(router_ref, column[0]).astype(F32)
            routed = jnp.zeros((TOK, COLS), F32)
            for e in range(EXPERTS):
                hit1 = ((lane == at1) & (first == e)).astype(F32)
                hit2 = ((lane == at2) & (second == e)).astype(F32)
                take = upper * hit1 + (1.0 - upper) * hit2
                high = take.astype(BF16)
                take_ref[0, e] = high
                take_ref[1, e] = (take - high.astype(F32)).astype(BF16)
                hits_ref[0, e] = take
                hits_ref[1, e] = hit1 - hit2
                sign = (first == e).astype(F32) - (second == e).astype(F32)
                routed = routed + sign * router[e : e + 1]
            routed_ref[...] = routed
    grad_down_ref[...] = grad_down
    grad_up_ref[...] = ADAPTER_SCALE * grad_up


def finish_kernel(column, in_ref, gain_ref, side_ref, base_ref, sb_ref, take_ref, hits_ref, routed_ref, out_ref):
    side = side_ref[...]
    scale, adapter_stat, raw, upper = (side[:, k : k + 1] for k in range(4))
    rows = jnp.zeros((TOK, COLS), F32)
    spread = jnp.zeros((TOK, 128), F32)
    stat = jnp.zeros((TOK, 128), F32)
    for e in range(EXPERTS):
        total = in_ref[stand(4 * e)].astype(F32)
        for k in range(1, 4):
            total = total + in_ref[stand(4 * e + k)].astype(F32)
        lines = total[CAP : CAP + 8] + total[CAP + 8 : CAP + 16]
        spread = spread + hits_ref[1, e] * (lines[0:1] + lines[2:3])
        stat = stat + hits_ref[0, e] * (lines[1:2] + lines[3:4])
        high, low = high_low(total[0:CAP])
        take = take_ref[0, e, :, 0:CAP]
        rows = rows + dot(take, high, 1, 0) + dot(take, low, 1, 0) + dot(take_ref[1, e, :, 0:CAP], high, 1, 0)
    delta = jnp.sum(spread, axis=1, keepdims=True) * upper * (1.0 - upper)
    stat = jnp.sum(stat, axis=1, keepdims=True) / scale + adapter_stat + delta * raw
    dnormed = rows + delta * routed_ref[...]
    result = base_ref[...] + scale * dnormed * local_columns(gain_ref, column[0]) - sb_ref[...] * stat
    out_ref[...] = result.astype(BF16)


VMEM = pl.BlockSpec(memory_space=pltpu.VMEM)
SMEM = pl.BlockSpec(memory_space=pltpu.SMEM)
HBM = pl.BlockSpec(memory_space=pltpu.HBM)


def pinned(v):
    return pltpu.with_memory_space_constraint(v, pltpu.HBM)


def call(kernel, out_shape, scalars, args, scratch=(), arg_specs=None):
    return pl.pallas_call(
        kernel,
        in_specs=[SMEM] * len(scalars) + (arg_specs or [VMEM] * len(args)),
        out_specs=VMEM if isinstance(out_shape, jax.ShapeDtypeStruct) else (VMEM,) * len(out_shape),
        out_shape=out_shape,
        scratch_shapes=scratch,
        compiler_params=pltpu.CompilerParams(vmem_limit_bytes=32 * 1024 * 1024),
    )(*scalars, *(pinned(v) if spec is HBM else v for v, spec in zip(args, arg_specs or [VMEM] * len(args))))


def shards(stash, cotangent, routes, lengths, gains, router, wg, wu, wd, down, up):
    x, g = stash[0], cotangent[0]
    routes, router, down = routes[0].T, router[0].T, down[0].T
    wg, wu, wd, up = wg[0], wu[0], wd[0], up[0]
    shape = jax.ShapeDtypeStruct
    column = lax.axis_index(EXPERT).astype(jnp.int32).reshape(1)
    block = lax.axis_index("dp").astype(jnp.int32).reshape(1)
    swap = [(0, 1), (1, 0)]
    locals_ = (lengths, x, g, routes, gains, router, down, up)
    sent, early, pair = call(
        prepare_kernel,
        (shape((GROUPS, SEND, 128), BF16), shape((EARLY, MODEL_WIDTH), BF16), shape((2, TOK, COLS), BF16)),
        (column, block),
        (*locals_, wd),
        [pltpu.SMEM(lengths.shape, jnp.int32)]
        + [pltpu.VMEM(v.shape, v.dtype) for v in locals_[1:]]
        + [pltpu.SemaphoreType.DMA((8 + EARLY // 128,))],
        [HBM] * 9,
    )
    own = lax.all_to_all(sent, EXCHANGE, 0, 0, tiled=True)
    other = lax.ppermute(own, "dp", swap)
    gains_here, *weights = call(
        weights_kernel,
        (
            shape(gains.shape, F32), shape(wg.shape, BF16), shape(wu.shape, BF16),
            shape((HIDDEN - EARLY, MODEL_WIDTH), BF16),
        ),
        (),
        (gains, wg, wu, wd),
        [pltpu.SemaphoreType.DMA((3, 4)), pltpu.SemaphoreType.DMA],
        [HBM] * 4,
    )
    other, pair = lax.optimization_barrier((other, lax.ppermute(pair, "dp", swap)))
    own_part, other_part = call(
        expert_kernel,
        (shape((GROUPS, BACK, 128), F32), shape((GROUPS, BACK, 128), BF16)),
        (),
        (own, other, gains_here, *weights, early),
        [
            pltpu.VMEM((2 * CAP, MODEL_WIDTH), BF16),
            pltpu.VMEM((2 * CAP, MODEL_WIDTH), BF16),
            pltpu.VMEM((2 * CAP, HIDDEN), BF16),
            pltpu.VMEM((2 * CAP, HIDDEN), BF16),
        ],
    )
    arrived = lax.ppermute(other_part, "dp", swap)
    small = shape((JOBS * RANK, COLS), F32)
    square = shape((TOK, COLS), F32)
    grad_down, grad_up, side, base, sb, take, hits, routed = call(
        stats_kernel,
        (
            small, small, square, square, square,
            shape((2, EXPERTS, TOK, 128), BF16), shape((2, EXPERTS, TOK, 128), F32), square,
        ),
        (column, block, lengths),
        (own, other, x, g, pair, routes, gains, down, router),
    )
    arrived, side = lax.optimization_barrier((arrived, side))
    parts = (own_part + arrived.astype(F32)).astype(BF16)
    back = lax.all_to_all(parts, EXCHANGE, 0, 0, tiled=True)
    result = call(
        finish_kernel,
        shape((TOK, COLS), BF16),
        (column,),
        (back, gains, side, base, sb, take, hits, routed),
    )
    count = lax.axis_size("section")
    handed = lax.ppermute(result, "section", [(i, (i - 1) % count) for i in range(count)])
    return handed[None], grad_down.T[None], grad_up[None]


def solution(mesh):
    finer = Mesh(
        mesh.devices.reshape(mesh.shape["section"], 4, 4, mesh.shape["dp"]),
        ("section", "expert_0", "expert_1", "dp"),
    )
    in_specs = (
        P("section", "dp", EXPERT),
        P("section", "dp", EXPERT),
        P("section", "dp", None),
        P("section", None),
        P("section", None),
        P("section", None, None),
        P("section", None, EXPERT_DP),
        P("section", None, EXPERT_DP),
        P("section", EXPERT_DP, None),
        P("section", EXPERT, None),
        P("section", None, EXPERT),
    )
    out_specs = (P("section", "dp", EXPERT), P("section", EXPERT, None), P("section", None, EXPERT))
    return jax.shard_map(shards, mesh=finer, in_specs=in_specs, out_specs=out_specs, check_vma=False)
```
